32 devices in a mesh: tbl: 8 (over z, y), pair: 4 (over x, core).
Axes of the slice: x: 2, y: 2, z: 4, core: 2. Of those that a mesh axis runs over, the one named last changes fastest.
Arguments:
- codes: bfloat16 [112, 64, 16384], P('tbl', None, 'pair'), may hold values from -127 to 127
- scales: float32 [112, 16384], P('tbl', 'pair'), may hold values from 0.002 to 0.02
- shard_slot: int32 [8, 14], replicated, may hold values from -1 to 53, as said below
- weight_first: bfloat16 [351, 1024], replicated, may hold values from -0.3125 to 0.3125
- bias_first: float32 [1024], replicated, may hold values from -3 to 3
- weight_second: bfloat16 [1024, 1024], replicated, may hold values from -0.1875 to 0.1875
- bias_second: float32 [1024], replicated, may hold values from -3 to 3
- weight_third: bfloat16 [1024, 512], replicated, may hold values from -0.1875 to 0.1875
- bias_third: float32 [512], replicated, may hold values from -3 to 3
- weight_fourth: bfloat16 [512, 256], replicated, may hold values from -0.25 to 0.25
- bias_fourth: float32 [256], replicated, may hold values from -3 to 3
- weight_out: bfloat16 [256], replicated, may hold values from -0.375 to 0.375
- bias_out: float32 [1], replicated, may hold values from -3 to 3
Outputs:
- logits: float32 [4, 4096], P(None, 'tbl')
The draws below stay inside these ranges and needn't reach their ends.
Inputs may be any that keep to these rules, and one draw needn't show every extreme that they name: `shard_slot`: each shard 0 to 53 stands in exactly one slot; all other slots hold -1. For k below half of the tbl size, row k holds its shards in its first slots and the row half the tbl size further holds its shards in its last slots, and the two rows hold 14 shards or fewer together. Some row holds 14 shards.
All inputs are finite; a program needn't handle non-finite values.
Results may differ from the reference program's by a relative error of at most 0.03.
Values may be sent and summed in bfloat16 or wider, within the bound.
No kernel may reach another device: no remote copies, remote signals or barrier semaphores. Data moves between devices by JAX's collectives and lax.ppermute only.
A program may use at most 128 MiB of HBM per device.

```python
import math
import jax
import jax.numpy as jnp
import numpy as np
from jax import lax

TABLES = 27
TOP_ONE = 1024
TOP_TWO = 1024
TOP_THREE = 512
TOP_FOUR = 256
HALF = 64
SHARDS = 54
PAIRS = 351
SLOTS = 14
BATCH_PAIR = 4096
BATCH = 16384
N_TBL = 8
N_PAIR = 4


def draw_shard_slot(key, part):
    span = N_TBL // 2
    key_rank, key_split, key_order = jax.random.split(jax.random.fold_in(key, 71), 3)
    rank = jax.random.permutation(key_rank, span).astype(jnp.int32)
    count = jnp.clip(SHARDS - rank * SLOTS, 0, SLOTS)
    lower = jax.random.randint(key_split, (span,), 0, SLOTS + 1)
    lower = jnp.minimum(lower, count)
    lower = jnp.where(rank == 0, count, lower)
    order = jax.random.permutation(key_order, SHARDS).astype(jnp.int32)
    padded = jnp.concatenate([order, jnp.zeros((span * SLOTS - SHARDS,), jnp.int32)])
    slot_index = jnp.arange(SLOTS, dtype=jnp.int32)
    low_place = rank[:, None] * SLOTS + slot_index[None, :]
    low_valid = slot_index[None, :] < lower[:, None]
    upper_count = count - lower
    upper_start = SLOTS - upper_count
    high_place = rank[:, None] * SLOTS + lower[:, None] + slot_index[None, :] - upper_start[:, None]
    high_valid = slot_index[None, :] >= upper_start[:, None]
    limit = span * SLOTS - 1
    low_rows = jnp.where(low_valid, padded[jnp.clip(low_place, 0, limit)], -1)
    high_rows = jnp.where(high_valid, padded[jnp.clip(high_place, 0, limit)], -1)
    return jnp.concatenate([low_rows, high_rows], axis=0).astype(jnp.int32)


def level_of(rng, extent, pieces, smallest, top_value):
    gain, own = 1.0, jax.random.fold_in(rng, 6)
    for dim, shards_of in pieces:
        heights = jnp.exp(jax.random.uniform(jax.random.fold_in(own, dim), (shards_of,), jnp.float32, smallest / len(pieces), top_value / len(pieces)))
        gain = gain * jnp.repeat(heights, extent[dim] // shards_of).reshape([-1 if axis == dim else 1 for axis in range(len(extent))])
    return gain


def gaussian(rng, dims, spread, reach, kind=jnp.bfloat16):
    array = spread * jax.random.normal(rng, dims, jnp.float32)
    return jnp.clip(array, min=-reach, max=reach).astype(kind)


def setup_inputs(seed: int = 0) -> dict:
    arg_keys = jax.random.split(jax.random.key(seed), 14)
    codes = jnp.clip(jax.random.uniform(arg_keys[0], (N_TBL * SLOTS, HALF, BATCH), jnp.float32, -127.0, 127.0) * level_of(arg_keys[0], (N_TBL * SLOTS, HALF, BATCH), ((0, 8), (2, 4)), -0.4, 0.0), -127.0, 127.0).astype(jnp.bfloat16)
    scales = jnp.clip(jnp.exp(math.log(0.02) - 2.30258502 * jax.random.uniform(arg_keys[1], (N_TBL * SLOTS, BATCH), jnp.float32) ** level_of(arg_keys[1], (N_TBL * SLOTS, BATCH), ((0, 8), (1, 4)), -0.2, 0.2)), 0.002, 0.02)
    shard_slot = draw_shard_slot(jax.random.fold_in(arg_keys[13], 71), 0)
    weight_first = gaussian(arg_keys[3], (PAIRS, TOP_ONE), PAIRS ** -0.5, 0.3125)
    bias_first = gaussian(arg_keys[4], (TOP_ONE,), 0.5, 3.0, jnp.float32)
    weight_second = gaussian(arg_keys[5], (TOP_ONE, TOP_TWO), TOP_ONE ** -0.5, 0.1875)
    bias_second = gaussian(arg_keys[6], (TOP_TWO,), 0.5, 3.0, jnp.float32)
    weight_third = gaussian(arg_keys[7], (TOP_TWO, TOP_THREE), TOP_TWO ** -0.5, 0.1875)
    bias_third = gaussian(arg_keys[8], (TOP_THREE,), 0.5, 3.0, jnp.float32)
    weight_fourth = gaussian(arg_keys[9], (TOP_THREE, TOP_FOUR), TOP_THREE ** -0.5, 0.25)
    bias_fourth = gaussian(arg_keys[10], (TOP_FOUR,), 0.5, 3.0, jnp.float32)
    weight_out = gaussian(arg_keys[11], (TOP_FOUR,), TOP_FOUR ** -0.5, 0.375)
    bias_out = gaussian(arg_keys[12], (1,), 1.0, 3.0, jnp.float32)
    return dict(codes=codes, scales=scales, shard_slot=shard_slot, weight_first=weight_first, bias_first=bias_first, weight_second=weight_second, bias_second=bias_second, weight_third=weight_third, bias_third=bias_third, weight_fourth=weight_fourth, bias_fourth=bias_fourth, weight_out=weight_out, bias_out=bias_out)


def pair_columns(tables):
    first, second = np.triu_indices(tables, 1)
    return (first * tables + second).astype(np.int32)


def shard_positions(slot_table, shard_total):
    flat = slot_table.reshape(-1)
    matches = flat[None, :] == jnp.arange(shard_total, dtype=jnp.int32)[:, None]
    places = jnp.arange(flat.shape[0], dtype=jnp.int32)[None, :]
    return jnp.sum(jnp.where(matches, places, 0), axis=1).astype(jnp.int32)


def dense_layer(inputs, weight, bias):
    product = jnp.dot(inputs.astype(jnp.float32), weight.astype(jnp.float32), precision=lax.Precision.HIGHEST)
    return jax.nn.relu(product + bias).astype(jnp.bfloat16)


def score_samples(picked_codes, picked_scales, layers):
    values = picked_codes.astype(jnp.float32) * picked_scales[:, None, :]
    table_count = values.shape[0] // 2
    count = values.shape[2]
    values = values.reshape(table_count, 2 * values.shape[1], count)
    gram = jnp.einsum("idb,jdb->bij", values, values, precision=lax.Precision.HIGHEST)
    flat = gram.reshape(count, table_count * table_count)
    hidden = flat[:, pair_columns(table_count)].astype(jnp.bfloat16)
    for weight, bias in layers[:-1]:
        hidden = dense_layer(hidden, weight, bias)
    weight_last, bias_last = layers[-1]
    final = jnp.dot(hidden.astype(jnp.float32), weight_last.astype(jnp.float32), precision=lax.Precision.HIGHEST)
    return final + bias_last[0]


def reference(codes, scales, shard_slot, weight_first, bias_first, weight_second, bias_second, weight_third, bias_third, weight_fourth, bias_fourth, weight_out, bias_out):
    layers = ((weight_first, bias_first), (weight_second, bias_second), (weight_third, bias_third), (weight_fourth, bias_fourth), (weight_out, bias_out))
    positions = shard_positions(shard_slot, 2 * TABLES)
    picked_codes = jnp.take(codes, positions, axis=0)
    picked_scales = jnp.take(scales, positions, axis=0)

    def block(index):
        start = index * BATCH_PAIR
        block_codes = lax.dynamic_slice_in_dim(picked_codes, start, BATCH_PAIR, 2)
        block_scales = lax.dynamic_slice_in_dim(picked_scales, start, BATCH_PAIR, 1)
        return score_samples(block_codes, block_scales, layers)

    logits = lax.map(block, jnp.arange(BATCH // BATCH_PAIR, dtype=jnp.int32))
    return logits.reshape(N_PAIR, BATCH_PAIR)
```

```python
import functools
import jax
import jax.numpy as jnp
import numpy as np
from jax import lax
from jax.sharding import PartitionSpec as P
from jax.experimental import pallas as pl
from jax.experimental.pallas import tpu as pltpu

LANES = 128


def pad_to(count, step):
    return -(-count // step) * step


def score_kernel(pos_ref, pool_ref, w1_ref, w2_ref, w3_ref, w4_ref, b1_ref, b2_ref, b3_ref, b4_ref, wo_ref, bo_ref,
                 out_ref, picked, wide, inter, w1, w2, w3, w4, pick_sem, weight_sem):
    shards, half, count = picked.shape
    tables = shards // 2
    weights = [
        pltpu.make_async_copy(src, dst, weight_sem.at[n])
        for n, (src, dst) in enumerate(((w1_ref, w1), (w2_ref, w2), (w3_ref, w3), (w4_ref, w4)))
    ]

    def fetch(shard):
        return pltpu.make_async_copy(pool_ref.at[pos_ref[shard]], picked.at[shard], pick_sem)

    def begin(shard, carry):
        fetch(shard).start()
        return carry

    def finish(shard, carry):
        fetch(shard).wait()
        return carry

    lax.fori_loop(0, shards, begin, 0)
    for copy in weights:
        copy.start()
    lax.fori_loop(0, shards, finish, 0)
    pairs = tables * (tables - 1) // 2
    rows = inter.shape[0]
    if rows > pairs:
        inter[pl.ds(pairs // 8 * 8, rows - pairs // 8 * 8), :] = jnp.zeros((rows - pairs // 8 * 8, count), jnp.float32)

    def gram_block(block, carry):
        lanes = pl.ds(pl.multiple_of(block * LANES, LANES), LANES)
        for shard in range(shards):
            wide[shard // 2, (shard % 2) * half:(shard % 2 + 1) * half, :] = picked[shard, :, lanes].astype(jnp.float32)
        row = 0
        for i in range(tables):
            left = wide[i]
            for j in range(i + 1, tables):
                inter[row:row + 1, lanes] = jnp.sum(left * wide[j], axis=0, keepdims=True)
                row += 1
        return carry

    lax.fori_loop(0, count // LANES, gram_block, 0)
    for copy in weights:
        copy.wait()
    step = 2 * LANES if count % (2 * LANES) == 0 else LANES

    def dense(hidden, weight, bias):
        product = jnp.dot(hidden, weight[...], preferred_element_type=jnp.float32)
        return jnp.maximum(product + bias[...], 0.0).astype(jnp.bfloat16)

    def top_block(block, carry):
        lanes = pl.ds(pl.multiple_of(block * step, step), step)
        hidden = jnp.transpose(inter[:, lanes]).astype(jnp.bfloat16)
        hidden = dense(hidden, w1, b1_ref)
        hidden = dense(hidden, w2, b2_ref)
        hidden = dense(hidden, w3, b3_ref)
        hidden = dense(hidden, w4, b4_ref)
        final = lax.dot_general(wo_ref[...], hidden, (((1,), (1,)), ((), ())), preferred_element_type=jnp.float32)
        out_ref[:, lanes] = final[0:1] + bo_ref[...]
        return carry

    lax.fori_loop(0, count // step, top_block, 0)


def score(pool, positions, layers):
    (w1, b1), (w2, b2), (w3, b3), (w4, b4), (wo, bo) = layers
    half, count = pool.shape[1:]
    shards = positions.shape[0]
    rows = pad_to(w1.shape[0], LANES)
    w1 = jnp.pad(w1, ((0, rows - w1.shape[0]), (0, 0)))
    wo = jnp.pad(wo[None, :], ((0, 7), (0, 0)))
    anywhere = pl.BlockSpec(memory_space=pl.ANY)
    vmem = pl.BlockSpec(memory_space=pltpu.VMEM)
    flops = 2 * count * sum(w.size for w in (w1, w2, w3, w4))
    return pl.pallas_call(
        score_kernel,
        out_shape=jax.ShapeDtypeStruct((1, count), jnp.float32),
        grid_spec=pltpu.PrefetchScalarGridSpec(
            num_scalar_prefetch=1,
            grid=(),
            in_specs=[anywhere] * 5 + [vmem] * 6,
            out_specs=vmem,
            scratch_shapes=[
                pltpu.VMEM((shards, half, count), pool.dtype),
                pltpu.VMEM((shards // 2, 2 * half, LANES), jnp.float32),
                pltpu.VMEM((rows, count), jnp.float32),
                pltpu.VMEM(w1.shape, w1.dtype),
                pltpu.VMEM(w2.shape, w2.dtype),
                pltpu.VMEM(w3.shape, w3.dtype),
                pltpu.VMEM(w4.shape, w4.dtype),
                pltpu.SemaphoreType.DMA,
                pltpu.SemaphoreType.DMA((4,)),
            ],
        ),
        compiler_params=pltpu.CompilerParams(vmem_limit_bytes=40 << 20),
        cost_estimate=pl.CostEstimate(flops=flops, bytes_accessed=shards * half * count * 2, transcendentals=0),
        name="score",
    )(positions, pool, w1, w2, w3, w4, b1[None, :], b2[None, :], b3[None, :], b4[None, :], wo, bo[None, :])


TABLES = 27


def shard_positions(slot_table, shard_total):
    flat = slot_table.reshape(-1)
    matches = flat[None, :] == jnp.arange(shard_total, dtype=jnp.int32)[:, None]
    places = jnp.arange(flat.shape[0], dtype=jnp.int32)[None, :]
    return jnp.sum(jnp.where(matches, places, 0), axis=1)


def per_device(codes, scales, shard_slot, *parameters):
    layers = tuple(zip(parameters[0::2], parameters[1::2]))
    slot_count, half, samples = codes.shape
    tbl_count = lax.axis_size("tbl")
    count = samples // tbl_count
    values = (codes.astype(jnp.float32) * scales[:, None, :]).astype(jnp.bfloat16)
    packed = values.reshape(slot_count, half, tbl_count, count).transpose(2, 0, 1, 3)
    received = lax.all_to_all(packed, "tbl", split_axis=0, concat_axis=0, tiled=True)
    pool = received.reshape(tbl_count * slot_count, half, count)
    positions = shard_positions(shard_slot, 2 * TABLES)
    logits = score(pool, positions, layers)
    return lax.all_gather(logits, "pair", axis=0, tiled=True)


def solution(mesh):
    return jax.shard_map(
        per_device,
        mesh=mesh,
        in_specs=(P("tbl", None, "pair"), P("tbl", "pair")) + (P(),) * 11,
        out_specs=P(None, "tbl"),
        check_vma=False,
    )
```

```python
import functools
import jax
import jax.numpy as jnp
import numpy as np
from jax import lax
from jax.experimental import pallas as pl
from jax.experimental.pallas import tpu as pltpu
from jax.sharding import PartitionSpec as P

TABLES = 27
LANES = 128
CHUNK = 6
ROUND_STEPS = (13, 14, 16)
LAG = 2
PIECE_ROUND = (4, 6, 8, 11)
SPAN = 256


def piece_order(nodes, node):
    if node < nodes // 2:
        return tuple(range(nodes - 1, node, -1)) + tuple(range(node)) + (node,)
    return tuple(range(node)) + tuple(range(nodes - 1, node, -1)) + (node,)


def whole_chunks(value):
    return (value * (-(-65536 // CHUNK))) >> 16


class Codes:
    def __init__(self, nodes, slots):
        self.nodes, self.slots = nodes, slots
        self.piece = 2 * nodes * slots
        self.pool = self.piece + nodes * slots
        self.units = nodes * nodes * slots
        self.stage = self.pool + self.units
        self.pool_rows = self.units + 2 * CHUNK


def plan_kernel(code, slot_ref, me_ref, out_ref):
    nodes, slots = code.nodes, code.slots
    half = nodes // 2
    me = me_ref[0]
    column, node = me & 1, me >> 1
    counts = []
    for row in range(2 * nodes):
        total = jnp.int32(0)
        for slot in range(slots):
            total += (slot_ref[row, slot] >= 0).astype(jnp.int32)
        counts.append(total)
    rows = {}
    for place in range(nodes):
        for other in range(2):
            row = column if other == 0 else 1 - column
            count = jnp.where(row == 0, counts[2 * place], counts[2 * place + 1])
            first = 0 if place < half else slots - count
            rows[place, other] = (count, first, ((place % half) * 2 + row) * slots)

    lists, ends = {}, []
    for up in (True, False):
        starts = {}
        path = range(nodes - 1) if up else range(nodes - 1, 0, -1)
        for place in path:
            goals = range(nodes - 1, place, -1) if up else range(place)
            before = range(place - 1, -1, -1) if up else range(place + 1, nodes)
            pieces = piece_order(nodes, place)
            items = [(source, other, goal) for other in range(2) for goal in goals for source in (place, *before)]
            end, here, segments = jnp.int32(0), {}, []
            for source, other, goal in items:
                count, first, base = rows[source, other]
                if source != place:
                    ready = starts[source, other, goal] + LAG * CHUNK
                elif other:
                    ready = jnp.int32(PIECE_ROUND[pieces.index(goal)] * CHUNK)
                else:
                    ready = jnp.int32(0)
                start = jnp.maximum(end, ready)
                segments.append((source, other, goal, start, starts.get((source, other, goal))))
                here[source, other, goal] = start
                end = jnp.where(count > 0, start + count, end)
            lists[up, place] = segments
            ends.append(end)
            starts = here
    last = functools.reduce(jnp.maximum, ends)

    spot = lax.broadcasted_iota(jnp.int32, (1, SPAN), 1)
    turn_of = whole_chunks(spot)
    rest = spot - turn_of * CHUNK
    tables = {}
    for (up, place), segments in lists.items():
        side = place % 2 if up else (place - 1) % 2
        came = 1 - side
        send = jnp.zeros((1, SPAN), jnp.int32)
        unit = code.units + side * CHUNK + rest
        for source, other, goal, start, earlier in segments:
            count, first, base = rows[source, other]
            index = spot - start
            inside = (index >= 0) & (index < count)
            slot = first + index
            this = goal * nodes * slots + base + slot
            if source != place:
                arrived = earlier + index
                came_in = whole_chunks(arrived)
                staged = code.stage + came * CHUNK + arrived - came_in * CHUNK
                origin = jnp.where(turn_of - came_in == LAG, staged, code.pool + this)
            elif other:
                origin = code.piece + piece_order(nodes, place).index(goal) * slots + slot
            else:
                origin = (goal * 2 + column) * slots + slot
            send = jnp.where(inside, origin, send)
            unit = jnp.where(inside, this, unit)
        tables[up, place] = (send, unit)
    blank = jnp.zeros((1, SPAN), jnp.int32)
    for side in range(2):
        sent = blank
        kept = code.units + side * CHUNK + rest
        for place in range(nodes):
            up = place % 2 == side
            peer = place + 1 if up else place - 1
            if 0 <= peer < nodes:
                sent = jnp.where(node == place, tables[up, place][0], sent)
                kept = jnp.where(node == place, tables[not up, peer][1], kept)
        out_ref[side:side + 1, :] = sent
        out_ref[2 + side:3 + side, :] = kept
    out_ref[4:5, :] = blank + lax.div(last + CHUNK - 1, jnp.int32(CHUNK))
    places = blank
    for row in range(2 * nodes):
        base = code.pool + (node * nodes + row % nodes) * slots
        base = jnp.where(row == (me ^ 1), code.piece, base)
        base = jnp.where(row == me, me * slots, base)
        for slot in range(slots):
            places = jnp.where(spot == slot_ref[row, slot], base + slot, places)
    out_ref[5:6, :] = places
    out_ref[6:8, :] = jnp.zeros((2, SPAN), jnp.int32)


def plan(shard_slot, me, code):
    return pl.pallas_call(
        functools.partial(plan_kernel, code),
        out_shape=jax.ShapeDtypeStruct((8, SPAN), jnp.int32),
        in_specs=[pl.BlockSpec(memory_space=pltpu.SMEM)] * 2,
        out_specs=pl.BlockSpec(memory_space=pltpu.VMEM),
        name="plan",
    )(shard_slot, me)


def turn_kernel(code, n_pieces, has_pool, has_recv, table_ref, round_ref, codes_ref, scales_ref, *refs):
    refs = list(refs)
    pieces = [refs.pop(0) for _ in range(n_pieces)]
    if has_pool:
        refs.pop(0)
    recvs = [refs.pop(0) for _ in range(2)] if has_recv else []
    pool_ref, send_a, send_b, buf, out, load_sem, recv_sem, pool_sem, send_sem = refs
    slots = code.slots
    units, half, count = out.shape
    base = round_ref[0] * CHUNK

    loads = [pltpu.make_async_copy(recvs[s], buf.at[pl.ds(units + s * CHUNK, CHUNK)], recv_sem.at[s]) for s in range(len(recvs))]
    for copy in loads:
        copy.start()

    def gather(side, c, carry):
        u = side * CHUNK + c
        e = table_ref[side, base + c]

        @pl.when(e < code.piece)
        def _():
            dest = lax.div(e, jnp.int32(slots))
            lanes = pl.ds(pl.multiple_of(dest * count, count), count)
            pltpu.make_async_copy(codes_ref.at[e - dest * slots, :, lanes], buf.at[u], load_sem).start()

        for n, piece in enumerate(pieces):
            low = code.piece + n * slots

            @pl.when((e >= low) & (e < low + slots))
            def _():
                pltpu.make_async_copy(piece.at[e - low], buf.at[u], load_sem).start()

        if has_recv:
            @pl.when((e >= code.pool) & (e < code.stage))
            def _():
                pltpu.make_async_copy(pool_ref.at[e - code.pool], buf.at[u], load_sem).start()

        return carry

    def gathered(side, c, carry):
        @pl.when(table_ref[side, base + c] < code.stage)
        def _():
            pltpu.make_async_copy(codes_ref.at[0, :, pl.ds(0, count)], buf.at[side * CHUNK + c], load_sem).wait()

        return carry

    for side in range(2):
        lax.fori_loop(0, CHUNK, functools.partial(gather, side), 0)
    for copy in loads:
        copy.wait()
    for side in range(2):
        lax.fori_loop(0, CHUNK, functools.partial(gathered, side), 0)

    def keep(side, c, carry):
        row = table_ref[2 + side, base - LAG * CHUNK + c]
        pltpu.make_async_copy(buf.at[units + side * CHUNK + c], pool_ref.at[row], pool_sem).start()
        return carry

    def kept(c, carry):
        pltpu.make_async_copy(buf.at[0], pool_ref.at[0], pool_sem).wait()
        return carry

    if has_recv:
        for side in range(2):
            lax.fori_loop(0, CHUNK, functools.partial(keep, side), 0)

    def scale(side, c, carry):
        u = side * CHUNK + c
        e = table_ref[side, base + c]
        own = e < code.piece
        dest = lax.div(e, jnp.int32(slots))
        place = jnp.where(e >= code.stage, units + e - code.stage, u)
        slot = jnp.where(own, e - dest * slots, 0)
        start = pl.multiple_of(jnp.where(own, dest, 0) * count, count)
        factor = jnp.where(own, scales_ref[pl.ds(slot, 1), pl.ds(start, count)], 1.0)
        out[u] = (buf[place].astype(jnp.float32) * factor).astype(out.dtype)
        return carry

    sends = []
    for side, ref in enumerate((send_a, send_b)):
        lax.fori_loop(0, CHUNK, functools.partial(scale, side), 0)
        sends.append(pltpu.make_async_copy(out.at[pl.ds(side * CHUNK, CHUNK)], ref, send_sem.at[side]))
        sends[-1].start()
    for copy in sends:
        copy.wait()
    if has_recv:
        lax.fori_loop(0, units, kept, 0)


def turn(code, table, number, codes, scales, pieces, pool, recv, count):
    half = codes.shape[1]
    anywhere = pl.BlockSpec(memory_space=pl.ANY)
    block = jax.ShapeDtypeStruct((CHUNK, half, count), codes.dtype)
    operands = [codes, scales, *pieces] + ([] if pool is None else [pool]) + list(recv or ())
    specs = [anywhere, pl.BlockSpec(memory_space=pltpu.VMEM)] + [anywhere] * (len(operands) - 2)
    aliases = {} if pool is None else {2 + 2 + len(pieces): 0}
    size = CHUNK * half * count * 2
    return pl.pallas_call(
        functools.partial(turn_kernel, code, len(pieces), pool is not None, recv is not None),
        out_shape=(jax.ShapeDtypeStruct((code.pool_rows, half, count), codes.dtype), block, block),
        grid_spec=pltpu.PrefetchScalarGridSpec(
            num_scalar_prefetch=2,
            grid=(),
            in_specs=specs,
            out_specs=(anywhere, anywhere, anywhere),
            scratch_shapes=[
                pltpu.VMEM((4 * CHUNK, half, count), codes.dtype),
                pltpu.VMEM((2 * CHUNK, half, count), codes.dtype),
                pltpu.SemaphoreType.DMA,
                pltpu.SemaphoreType.DMA((2,)),
                pltpu.SemaphoreType.DMA,
                pltpu.SemaphoreType.DMA((2,)),
            ],
        ),
        input_output_aliases=aliases,
        cost_estimate=pl.CostEstimate(flops=size, bytes_accessed=8 * size, transcendentals=0),
        name="turn",
    )(table, number, *operands)


def settle_kernel(table_ref, round_ref, pool_in, recv_a, recv_b, pool_ref, buf, load_sem, pool_sem):
    base = round_ref[0] * CHUNK
    loads = [pltpu.make_async_copy(ref, buf.at[pl.ds(n * CHUNK, CHUNK)], load_sem.at[n]) for n, ref in enumerate((recv_a, recv_b))]
    for copy in loads:
        copy.start()
    stores = []
    for n in range(2):
        loads[n].wait()
        for c in range(CHUNK):
            row = table_ref[2 + n, base + c]
            stores.append(pltpu.make_async_copy(buf.at[n * CHUNK + c], pool_ref.at[row], pool_sem))
            stores[-1].start()
    for copy in stores:
        copy.wait()


def settle(table, number, pool, recv):
    anywhere = pl.BlockSpec(memory_space=pl.ANY)
    return pl.pallas_call(
        settle_kernel,
        out_shape=jax.ShapeDtypeStruct(pool.shape, pool.dtype),
        grid_spec=pltpu.PrefetchScalarGridSpec(
            num_scalar_prefetch=2,
            grid=(),
            in_specs=[anywhere] * 3,
            out_specs=anywhere,
            scratch_shapes=[
                pltpu.VMEM((2 * CHUNK,) + pool.shape[1:], pool.dtype),
                pltpu.SemaphoreType.DMA((2,)),
                pltpu.SemaphoreType.DMA,
            ],
        ),
        input_output_aliases={2: 0},
        name="settle",
    )(table, number, pool, *recv)


def score_kernel(limits, pos_ref, pool_ref, codes_ref, piece_ref, scales_ref, w1_ref, w2_ref, w3_ref, w4_ref, b1_ref, b2_ref, b3_ref, b4_ref, wo_ref, bo_ref,
                 out_ref, picked, wide, inter, w1, w2, w3, w4, pick_sem, weight_sem):
    shards, half, count = picked.shape
    tables = shards // 2
    weights = [
        pltpu.make_async_copy(src, dst, weight_sem.at[n])
        for n, (src, dst) in enumerate(((w1_ref, w1), (w2_ref, w2), (w3_ref, w3), (w4_ref, w4)))
    ]

    slots, piece_base, pool_base, table_row = limits

    def begin(shard, carry):
        e = pos_ref[table_row, shard]
        dest = lax.div(e, jnp.int32(slots))

        @pl.when(e < piece_base)
        def _():
            lanes = pl.ds(pl.multiple_of(dest * count, count), count)
            pltpu.make_async_copy(codes_ref.at[e - dest * slots, :, lanes], picked.at[shard], pick_sem).start()

        @pl.when((e >= piece_base) & (e < pool_base))
        def _():
            pltpu.make_async_copy(piece_ref.at[e - piece_base], picked.at[shard], pick_sem).start()

        @pl.when(e >= pool_base)
        def _():
            pltpu.make_async_copy(pool_ref.at[e - pool_base], picked.at[shard], pick_sem).start()

        return carry

    def finish(shard, carry):
        pltpu.make_async_copy(pool_ref.at[0], picked.at[shard], pick_sem).wait()
        return carry

    def rescale(shard, carry):
        e = pos_ref[table_row, shard]
        dest = lax.div(e, jnp.int32(slots))

        @pl.when(e < piece_base)
        def _():
            lanes = pl.ds(pl.multiple_of(dest * count, count), count)
            factor = scales_ref[pl.ds(e - dest * slots, 1), lanes]
            picked[shard] = (picked[shard].astype(jnp.float32) * factor).astype(picked.dtype)

        return carry

    lax.fori_loop(0, shards, begin, 0)
    for copy in weights:
        copy.start()
    lax.fori_loop(0, shards, finish, 0)
    lax.fori_loop(0, shards, rescale, 0)
    def gram_block(block, carry):
        lanes = pl.ds(pl.multiple_of(block * LANES, LANES), LANES)
        for shard in range(shards):
            wide[shard // 2, (shard % 2) * half:(shard % 2 + 1) * half, :] = picked[shard, :, lanes].astype(jnp.float32)
        row = 0
        for i in range(tables):
            left = wide[i]
            for j in range(i + 1, tables):
                inter[row:row + 1, lanes] = jnp.sum(left * wide[j], axis=0, keepdims=True)
                row += 1
        return carry

    lax.fori_loop(0, count // LANES, gram_block, 0)
    for copy in weights:
        copy.wait()
    step = 2 * LANES if count % (2 * LANES) == 0 else LANES

    def dense(hidden, weight, bias):
        product = jnp.dot(hidden, weight[...], preferred_element_type=jnp.float32)
        return jnp.maximum(product + bias[...], 0.0).astype(jnp.bfloat16)

    def top_block(block, carry):
        lanes = pl.ds(pl.multiple_of(block * step, step), step)
        hidden = jnp.transpose(inter[:, lanes]).astype(jnp.bfloat16)
        hidden = dense(hidden, w1, b1_ref)
        hidden = dense(hidden, w2, b2_ref)
        hidden = dense(hidden, w3, b3_ref)
        hidden = dense(hidden, w4, b4_ref)
        final = lax.dot_general(wo_ref[...], hidden, (((1,), (1,)), ((), ())), preferred_element_type=jnp.float32)
        out_ref[:, lanes] = final[0:1] + bo_ref[...]
        return carry

    lax.fori_loop(0, count // step, top_block, 0)


def score(pool, codes, piece, scales, positions, shards, limits, layers):
    (w1, b1), (w2, b2), (w3, b3), (w4, b4), (wo, bo) = layers
    half, count = pool.shape[1:]
    rows = w1.shape[0]
    wo = wo[None, :]
    anywhere = pl.BlockSpec(memory_space=pl.ANY)
    vmem = pl.BlockSpec(memory_space=pltpu.VMEM)
    flops = 2 * count * sum(w.size for w in (w1, w2, w3, w4))
    return pl.pallas_call(
        functools.partial(score_kernel, limits),
        out_shape=jax.ShapeDtypeStruct((1, count), jnp.float32),
        grid_spec=pltpu.PrefetchScalarGridSpec(
            num_scalar_prefetch=1,
            grid=(),
            in_specs=[anywhere] * 3 + [vmem] + [pl.BlockSpec(memory_space=pltpu.HBM)] * 4 + [vmem] * 6,
            out_specs=vmem,
            scratch_shapes=[
                pltpu.VMEM((shards, half, count), pool.dtype),
                pltpu.VMEM((shards // 2, 2 * half, LANES), jnp.float32),
                pltpu.VMEM((rows, count), jnp.float32),
                pltpu.VMEM(w1.shape, w1.dtype),
                pltpu.VMEM(w2.shape, w2.dtype),
                pltpu.VMEM(w3.shape, w3.dtype),
                pltpu.VMEM(w4.shape, w4.dtype),
                pltpu.SemaphoreType.DMA,
                pltpu.SemaphoreType.DMA((4,)),
            ],
        ),
        compiler_params=pltpu.CompilerParams(vmem_limit_bytes=40 << 20),
        cost_estimate=pl.CostEstimate(flops=flops, bytes_accessed=shards * half * count * 2, transcendentals=0),
        name="score",
    )(positions, pool, codes, piece, scales, w1, w2, w3, w4, b1[None, :], b2[None, :], b3[None, :], b4[None, :], wo, bo[None, :])


def shard_positions(slot_table, shard_total):
    flat = slot_table.reshape(-1)
    matches = flat[None, :] == jnp.arange(shard_total, dtype=jnp.int32)[:, None]
    places = jnp.arange(flat.shape[0], dtype=jnp.int32)[None, :]
    return jnp.sum(jnp.where(matches, places, 0), axis=1)


def exchange_all(codes, scales):
    slot_count, half, samples = codes.shape
    tbl_count = lax.axis_size("tbl")
    count = samples // tbl_count
    values = (codes.astype(jnp.float32) * scales[:, None, :]).astype(codes.dtype)
    packed = values.reshape(slot_count, half, tbl_count, count).transpose(2, 0, 1, 3)
    received = lax.all_to_all(packed, "tbl", split_axis=0, concat_axis=0, tiled=True)
    return received.reshape(tbl_count * slot_count, half, count)


def exchange_line(code, codes, scales, shard_slot):
    nodes, slots = code.nodes, code.slots
    half, samples = codes.shape[1:]
    count = samples // (2 * nodes)
    me = lax.axis_index("tbl")
    column, node = me & 1, me >> 1
    table = plan(shard_slot, me.astype(jnp.int32)[None], code)
    rounds = table[4, 0]

    def index(place, col):
        return place * 2 + col

    swaps = []
    for side in range(2):
        pairs = [(index(a, c), index(a + 1, c)) for a in range(side, nodes - 1, 2) for c in range(2)]
        swaps.append(pairs + [(b, a) for a, b in pairs])
    across = [(index(a, c), index(a, 1 - c)) for a in range(nodes) for c in range(2)]
    orders = np.array([piece_order(nodes, place) for place in range(nodes)], np.int32)

    def piece(n, after):
        goal = jnp.int32(0)
        for place in range(nodes):
            goal = jnp.where(node == place, int(orders[place, n]), goal)
        start, _ = lax.optimization_barrier(((goal * 2 + 1 - column) * count, after))
        part = lax.dynamic_slice_in_dim(codes, start, count, 2).astype(jnp.float32)
        factor = lax.dynamic_slice_in_dim(scales, start, count, 1)
        return lax.ppermute((part * factor[:, None, :]).astype(codes.dtype), "tbl", across)

    def number(value):
        return jnp.full((1,), value, jnp.int32)

    def swap(sends):
        return [lax.ppermute(sent, "tbl", pairs) for sent, pairs in zip(sends, swaps)]

    def run(limit, open_end):
        pool, arrived, pieces = None, [], []
        for r in range(limit):
            ready = [p for n, p in enumerate(pieces[:-1]) if PIECE_ROUND[n] <= r]
            recv = arrived[r - LAG] if r >= LAG else None
            pool, *sends = turn(code, table, number(r), codes, scales, ready, pool, recv, count)
            if r < nodes:
                pieces.append(piece(r, sends[0]))
            arrived.append(swap(sends))
        final, early, late = jnp.int32(limit), arrived[-2], arrived[-1]
        if open_end:
            def step(state):
                r, pool, early, late = state
                pool, *sends = turn(code, table, r[None], codes, scales, pieces[:-1], pool, early, count)
                return r + 1, pool, late, swap(sends)

            final, pool, early, late = lax.while_loop(lambda state: state[0] < rounds, step, (final, pool, early, late))
        pool = settle(table, final[None] - 2, pool, early)
        return settle(table, final[None] - 1, pool, late), pieces[-1]

    steps = [functools.partial(run, limit, limit == ROUND_STEPS[-1]) for limit in ROUND_STEPS]
    choice = sum((rounds > limit).astype(jnp.int32) for limit in ROUND_STEPS[:-1])
    pool, piece_own = lax.switch(choice, steps)
    return table, pool, piece_own


def per_device(codes, scales, shard_slot, *parameters):
    layers = tuple(zip(parameters[0::2], parameters[1::2]))
    slots = codes.shape[0]
    tbl_count = lax.axis_size("tbl")
    shards = 2 * TABLES
    if tbl_count % 4 == 0 and slots >= tbl_count:
        code = Codes(tbl_count // 2, slots)
        places, pool, piece = exchange_line(code, codes, scales, shard_slot)
        limits = (slots, code.piece, code.pool, 5)
    else:
        pool = exchange_all(codes, scales)
        piece, places, limits = pool, shard_positions(shard_slot, shards)[None, :], (slots, 0, 0, 0)
    logits = score(pool, codes, piece, scales, places, shards, limits, layers)
    return lax.all_gather(logits, "pair", axis=0, tiled=True)


def solution(mesh):
    return jax.shard_map(
        per_device,
        mesh=mesh,
        in_specs=(P("tbl", None, "pair"), P("tbl", "pair")) + (P(),) * 11,
        out_specs=P(None, "tbl"),
        check_vma=False,
    )
```

```python
import functools
import jax
import jax.numpy as jnp
from jax import lax
from jax.experimental import pallas as pl
from jax.experimental.pallas import tpu as pltpu
from jax.sharding import PartitionSpec as P

TABLES = 27
LANES = 128
CHUNK = 6
ROUND_STEPS = (13, 14, 16)
LAG = 2
PIECE_ROUND = (4, 6, 8, 11)
SPAN = 256


def piece_order(nodes, node):
    if node < nodes // 2:
        return tuple(range(nodes - 1, node, -1)) + tuple(range(node)) + (node,)
    return tuple(range(node)) + tuple(range(nodes - 1, node, -1)) + (node,)


def whole_chunks(value):
    return (value * (-(-65536 // CHUNK))) >> 16


class Codes:
    def __init__(self, nodes, slots):
        self.nodes, self.slots = nodes, slots
        self.piece = 2 * nodes * slots
        self.pool = self.piece + nodes * slots
        self.units = nodes * nodes * slots
        self.stage = self.pool + self.units
        self.pool_rows = self.units + 2 * CHUNK


def time_lists(code, counts, column, ends):
    nodes, slots = code.nodes, code.slots
    half = nodes // 2
    rows = {}
    for place in range(nodes):
        for other in range(2):
            row = column if other == 0 else 1 - column
            count = jnp.where(row == 0, counts[2 * place], counts[2 * place + 1])
            first = 0 if place < half else slots - count
            rows[place, other] = (count, first, ((place % half) * 2 + row) * slots)

    lists = {}
    for up in (True, False):
        starts = {}
        path = range(nodes - 1) if up else range(nodes - 1, 0, -1)
        for place in path:
            goals = range(nodes - 1, place, -1) if up else range(place)
            before = range(place - 1, -1, -1) if up else range(place + 1, nodes)
            pieces = piece_order(nodes, place)
            items = [(source, other, goal) for other in range(2) for goal in goals for source in (place, *before)]
            end, here, segments = jnp.int32(0), {}, []
            for source, other, goal in items:
                count, first, base = rows[source, other]
                if source != place:
                    ready = starts[source, other, goal] + LAG * CHUNK
                elif other:
                    ready = jnp.int32(PIECE_ROUND[pieces.index(goal)] * CHUNK)
                else:
                    ready = jnp.int32(0)
                start = jnp.maximum(end, ready)
                segments.append((source, other, goal, start, starts.get((source, other, goal))))
                here[source, other, goal] = start
                end = jnp.where(count > 0, start + count, end)
            lists[up, place] = segments
            ends.append(end)
            starts = here
    return rows, lists


def plan_kernel(code, slot_ref, me_ref, out_ref):
    nodes, slots = code.nodes, code.slots
    me = me_ref[0]
    column, node = me & 1, me >> 1
    counts = []
    for row in range(2 * nodes):
        total = jnp.int32(0)
        for slot in range(slots):
            total += (slot_ref[row, slot] >= 0).astype(jnp.int32)
        counts.append(total)
    ends = []
    for flip in range(2):
        rows, lists = time_lists(code, counts, column ^ flip, ends)
        if flip == 0:
            own_rows, own_lists = rows, lists
    rows, lists = own_rows, own_lists
    last = functools.reduce(jnp.maximum, ends)

    spot = lax.broadcasted_iota(jnp.int32, (1, SPAN), 1)
    turn_of = whole_chunks(spot)
    rest = spot - turn_of * CHUNK
    tables = {}
    for (up, place), segments in lists.items():
        side = place % 2 if up else (place - 1) % 2
        came = 1 - side
        send = jnp.zeros((1, SPAN), jnp.int32)
        unit = code.units + side * CHUNK + rest
        for source, other, goal, start, earlier in segments:
            count, first, base = rows[source, other]
            index = spot - start
            inside = (index >= 0) & (index < count)
            slot = first + index
            this = goal * nodes * slots + base + slot
            if source != place:
                arrived = earlier + index
                came_in = whole_chunks(arrived)
                staged = code.stage + came * CHUNK + arrived - came_in * CHUNK
                origin = jnp.where(turn_of - came_in == LAG, staged, code.pool + this)
            elif other:
                origin = code.piece + piece_order(nodes, place).index(goal) * slots + slot
            else:
                origin = (goal * 2 + column) * slots + slot
            send = jnp.where(inside, origin, send)
            unit = jnp.where(inside, this, unit)
        tables[up, place] = (send, unit)
    blank = jnp.zeros((1, SPAN), jnp.int32)
    for side in range(2):
        sent = blank
        kept = code.units + side * CHUNK + rest
        for place in range(nodes):
            up = place % 2 == side
            peer = place + 1 if up else place - 1
            if 0 <= peer < nodes:
                sent = jnp.where(node == place, tables[up, place][0], sent)
                kept = jnp.where(node == place, tables[not up, peer][1], kept)
        out_ref[side:side + 1, :] = sent
        out_ref[2 + side:3 + side, :] = kept
    out_ref[4:5, :] = blank + lax.div(last + CHUNK - 1, jnp.int32(CHUNK))
    places = blank
    for row in range(2 * nodes):
        base = code.pool + (node * nodes + row % nodes) * slots
        base = jnp.where(row == (me ^ 1), code.piece, base)
        base = jnp.where(row == me, me * slots, base)
        for slot in range(slots):
            places = jnp.where(spot == slot_ref[row, slot], base + slot, places)
    out_ref[5:6, :] = places
    out_ref[6:8, :] = jnp.zeros((2, SPAN), jnp.int32)


def plan(shard_slot, me, code):
    return pl.pallas_call(
        functools.partial(plan_kernel, code),
        out_shape=jax.ShapeDtypeStruct((8, SPAN), jnp.int32),
        in_specs=[pl.BlockSpec(memory_space=pltpu.SMEM)] * 2,
        out_specs=pl.BlockSpec(memory_space=pltpu.VMEM),
        name="plan",
    )(shard_slot, me)


def rescale(block, scales_ref, slot, start, count):
    factor = scales_ref[pl.ds(slot, 1), pl.ds(pl.multiple_of(start, LANES), count)]
    return (block.astype(jnp.float32) * factor).astype(block.dtype)


def turn_kernel(code, n_pieces, has_pool, has_recv, base, table_ref, *refs):
    refs = list(refs)
    if base is None:
        base = refs.pop(0)[0] * CHUNK
    codes_ref, scales_ref = refs.pop(0), refs.pop(0)
    pieces = [refs.pop(0) for _ in range(n_pieces)]
    if has_pool:
        refs.pop(0)
    recvs = [refs.pop(0) for _ in range(2)] if has_recv else []
    pool_ref, send_a, send_b, buf, load_sem, recv_sem, pool_sem = refs
    slots = code.slots
    count = buf.shape[2]
    loads = [pltpu.make_async_copy(ref, buf.at[pl.ds(s * CHUNK, CHUNK)], recv_sem.at[s]) for s, ref in enumerate(recvs)]

    def gather(side, send, c, carry):
        e = table_ref[side, base + c]
        goal = send.at[c]

        @pl.when(e < code.piece)
        def _():
            dest = lax.div(e, jnp.int32(slots))
            lanes = pl.ds(pl.multiple_of(dest * count, count), count)
            pltpu.make_async_copy(codes_ref.at[e - dest * slots, :, lanes], goal, load_sem).start()

        if has_recv:
            @pl.when(e >= code.piece)
            def _():
                for n, piece in enumerate(pieces):
                    low = code.piece + n * slots

                    @pl.when((e >= low) & (e < low + slots))
                    def _():
                        pltpu.make_async_copy(piece.at[e - low], goal, load_sem).start()

                @pl.when((e >= code.pool) & (e < code.stage))
                def _():
                    pltpu.make_async_copy(pool_ref.at[e - code.pool], goal, load_sem).start()

                for n, recv in enumerate(recvs):
                    low = code.stage + n * CHUNK

                    @pl.when((e >= low) & (e < low + CHUNK))
                    def _():
                        pltpu.make_async_copy(recv.at[e - low], goal, load_sem).start()

        return carry

    def gathered(send, c, carry):
        pltpu.make_async_copy(codes_ref.at[0, :, pl.ds(0, count)], send.at[c], load_sem).wait()
        return carry

    def keep(side, c, carry):
        row = table_ref[2 + side, base - LAG * CHUNK + c]
        pltpu.make_async_copy(buf.at[side * CHUNK + c], pool_ref.at[row], pool_sem).start()
        return carry

    def kept(c, carry):
        pltpu.make_async_copy(buf.at[0], pool_ref.at[0], pool_sem).wait()
        return carry

    def scale(side, send, c, carry):
        e = table_ref[side, base + c]

        @pl.when(e < code.piece)
        def _():
            dest = lax.div(e, jnp.int32(slots))
            send[c] = rescale(send[c], scales_ref, e - dest * slots, dest * count, count)

        return carry

    sides = ((0, send_a), (1, send_b))
    for side, send in sides:
        lax.fori_loop(0, CHUNK, functools.partial(gather, side, send), 0)
    for copy in loads:
        copy.start()
    for side, send in sides:
        lax.fori_loop(0, CHUNK, functools.partial(gathered, send), 0)
    if has_recv:
        for side in range(2):
            loads[side].wait()
            lax.fori_loop(0, CHUNK, functools.partial(keep, side), 0)
    for side, send in sides:
        lax.fori_loop(0, CHUNK, functools.partial(scale, side, send), 0)
    if has_recv:
        lax.fori_loop(0, 2 * CHUNK, kept, 0)


def turn(code, table, number, codes, scales, pieces, pool, recv, count):
    half = codes.shape[1]
    anywhere = pl.BlockSpec(memory_space=pl.ANY)
    vmem = pl.BlockSpec(memory_space=pltpu.VMEM)
    block = jax.ShapeDtypeStruct((CHUNK, half, count), codes.dtype)
    operands = [codes, scales, *pieces] + ([] if pool is None else [pool]) + list(recv or ())
    specs = [anywhere, vmem] + [anywhere] * (len(operands) - 2)
    fixed = isinstance(number, int)
    scalars = (table,) if fixed else (table, number)
    aliases = {} if pool is None else {len(scalars) + 2 + len(pieces): 0}
    size = CHUNK * half * count * 2
    base = number * CHUNK if fixed else None
    return pl.pallas_call(
        functools.partial(turn_kernel, code, len(pieces), pool is not None, recv is not None, base),
        out_shape=(jax.ShapeDtypeStruct((code.pool_rows, half, count), codes.dtype), block, block),
        grid_spec=pltpu.PrefetchScalarGridSpec(
            num_scalar_prefetch=len(scalars),
            grid=(),
            in_specs=specs,
            out_specs=(anywhere, vmem, vmem),
            scratch_shapes=[
                pltpu.VMEM((2 * CHUNK, half, count), codes.dtype),
                pltpu.SemaphoreType.DMA,
                pltpu.SemaphoreType.DMA((2,)),
                pltpu.SemaphoreType.DMA,
            ],
        ),
        input_output_aliases=aliases,
        compiler_params=pltpu.CompilerParams(vmem_limit_bytes=8 << 20),
        cost_estimate=pl.CostEstimate(flops=size, bytes_accessed=8 * size, transcendentals=0),
        name="turn",
    )(*scalars, *operands)


def piece_kernel(nodes, n, me_ref, codes_ref, scales_ref, after_ref, out_ref, sem):
    me = me_ref[0]
    goal = jnp.int32(0)
    for place in range(nodes):
        goal = jnp.where((me >> 1) == place, piece_order(nodes, place)[n], goal)
    slots, half, count = out_ref.shape
    start = pl.multiple_of((goal * 2 + 1 - (me & 1)) * count, count)
    copy = pltpu.make_async_copy(codes_ref.at[:, :, pl.ds(start, count)], out_ref, sem)
    copy.start()
    copy.wait()

    def scale(slot, carry):
        out_ref[slot] = rescale(out_ref[slot], scales_ref, slot, start, count)
        return carry

    lax.fori_loop(0, slots, scale, 0)


def column_piece(nodes, n, me, codes, scales, after, count):
    slots, half, samples = codes.shape
    anywhere = pl.BlockSpec(memory_space=pl.ANY)
    vmem = pl.BlockSpec(memory_space=pltpu.VMEM)
    return pl.pallas_call(
        functools.partial(piece_kernel, nodes, n),
        out_shape=jax.ShapeDtypeStruct((slots, half, count), codes.dtype),
        grid_spec=pltpu.PrefetchScalarGridSpec(
            num_scalar_prefetch=1,
            grid=(),
            in_specs=[anywhere, vmem, anywhere],
            out_specs=vmem,
            scratch_shapes=[pltpu.SemaphoreType.DMA],
        ),
        compiler_params=pltpu.CompilerParams(vmem_limit_bytes=8 << 20),
        cost_estimate=pl.CostEstimate(flops=slots * half * count, bytes_accessed=4 * slots * half * count, transcendentals=0),
        name="piece",
    )(me, codes, scales, after)


def settle_kernel(table_ref, round_ref, pool_in, recv_a, recv_b, pool_ref, buf, load_sem, pool_sem):
    base = round_ref[0] * CHUNK
    loads = [pltpu.make_async_copy(ref, buf.at[pl.ds(n * CHUNK, CHUNK)], load_sem.at[n]) for n, ref in enumerate((recv_a, recv_b))]
    for copy in loads:
        copy.start()
    stores = []
    for n in range(2):
        loads[n].wait()
        for c in range(CHUNK):
            row = table_ref[2 + n, base + c]
            stores.append(pltpu.make_async_copy(buf.at[n * CHUNK + c], pool_ref.at[row], pool_sem))
            stores[-1].start()
    for copy in stores:
        copy.wait()


def settle(table, number, pool, recv):
    anywhere = pl.BlockSpec(memory_space=pl.ANY)
    return pl.pallas_call(
        settle_kernel,
        out_shape=jax.ShapeDtypeStruct(pool.shape, pool.dtype),
        grid_spec=pltpu.PrefetchScalarGridSpec(
            num_scalar_prefetch=2,
            grid=(),
            in_specs=[anywhere] * 3,
            out_specs=anywhere,
            scratch_shapes=[
                pltpu.VMEM((2 * CHUNK,) + pool.shape[1:], pool.dtype),
                pltpu.SemaphoreType.DMA((2,)),
                pltpu.SemaphoreType.DMA,
            ],
        ),
        input_output_aliases={2: 0},
        compiler_params=pltpu.CompilerParams(vmem_limit_bytes=8 << 20),
        name="settle",
    )(table, number, pool, *recv)


def score_kernel(limits, pos_ref, pool_ref, codes_ref, piece_ref, scales_ref, w1_ref, w2_ref, w3_ref, w4_ref, b1_ref, b2_ref, b3_ref, b4_ref, wo_ref, bo_ref,
                 out_ref, picked, wide, inter, w1, w2, w3, w4, pick_sem, weight_sem):
    shards, half, count = picked.shape
    tables = shards // 2
    weights = [
        pltpu.make_async_copy(src, dst, weight_sem.at[n])
        for n, (src, dst) in enumerate(((w1_ref, w1), (w2_ref, w2), (w3_ref, w3), (w4_ref, w4)))
    ]

    slots, piece_base, pool_base, table_row = limits

    def begin(shard, carry):
        e = pos_ref[table_row, shard]
        dest = lax.div(e, jnp.int32(slots))

        @pl.when(e < piece_base)
        def _():
            lanes = pl.ds(pl.multiple_of(dest * count, count), count)
            pltpu.make_async_copy(codes_ref.at[e - dest * slots, :, lanes], picked.at[shard], pick_sem).start()

        @pl.when((e >= piece_base) & (e < pool_base))
        def _():
            pltpu.make_async_copy(piece_ref.at[e - piece_base], picked.at[shard], pick_sem).start()

        @pl.when(e >= pool_base)
        def _():
            pltpu.make_async_copy(pool_ref.at[e - pool_base], picked.at[shard], pick_sem).start()

        return carry

    def finish(shard, carry):
        pltpu.make_async_copy(pool_ref.at[0], picked.at[shard], pick_sem).wait()
        return carry

    def rescale(shard, carry):
        e = pos_ref[table_row, shard]
        dest = lax.div(e, jnp.int32(slots))

        @pl.when(e < piece_base)
        def _():
            lanes = pl.ds(pl.multiple_of(dest * count, count), count)
            factor = scales_ref[pl.ds(e - dest * slots, 1), lanes]
            picked[shard] = (picked[shard].astype(jnp.float32) * factor).astype(picked.dtype)

        return carry

    lax.fori_loop(0, shards, begin, 0)
    for copy in weights:
        copy.start()
    lax.fori_loop(0, shards, finish, 0)
    lax.fori_loop(0, shards, rescale, 0)
    def gram_block(block, carry):
        lanes = pl.ds(pl.multiple_of(block * LANES, LANES), LANES)
        for shard in range(shards):
            wide[shard // 2, (shard % 2) * half:(shard % 2 + 1) * half, :] = picked[shard, :, lanes].astype(jnp.float32)
        row = 0
        for i in range(tables):
            left = wide[i]
            for j in range(i + 1, tables):
                inter[row:row + 1, lanes] = jnp.sum(left * wide[j], axis=0, keepdims=True)
                row += 1
        return carry

    lax.fori_loop(0, count // LANES, gram_block, 0)
    for copy in weights:
        copy.wait()
    step = 2 * LANES if count % (2 * LANES) == 0 else LANES

    def dense(hidden, weight, bias):
        product = jnp.dot(hidden, weight[...], preferred_element_type=jnp.float32)
        return jnp.maximum(product + bias[...], 0.0).astype(jnp.bfloat16)

    def top_block(block, carry):
        lanes = pl.ds(pl.multiple_of(block * step, step), step)
        hidden = jnp.transpose(inter[:, lanes]).astype(jnp.bfloat16)
        hidden = dense(hidden, w1, b1_ref)
        hidden = dense(hidden, w2, b2_ref)
        hidden = dense(hidden, w3, b3_ref)
        hidden = dense(hidden, w4, b4_ref)
        final = lax.dot_general(wo_ref[...], hidden, (((1,), (1,)), ((), ())), preferred_element_type=jnp.float32)
        out_ref[:, lanes] = final[0:1] + bo_ref[...]
        return carry

    lax.fori_loop(0, count // step, top_block, 0)


def score(pool, codes, piece, scales, positions, shards, limits, layers):
    (w1, b1), (w2, b2), (w3, b3), (w4, b4), (wo, bo) = layers
    half, count = pool.shape[1:]
    rows = w1.shape[0]
    wo = wo[None, :]
    anywhere = pl.BlockSpec(memory_space=pl.ANY)
    vmem = pl.BlockSpec(memory_space=pltpu.VMEM)
    flops = 2 * count * sum(w.size for w in (w1, w2, w3, w4))
    return pl.pallas_call(
        functools.partial(score_kernel, limits),
        out_shape=jax.ShapeDtypeStruct((1, count), jnp.float32),
        grid_spec=pltpu.PrefetchScalarGridSpec(
            num_scalar_prefetch=1,
            grid=(),
            in_specs=[anywhere] * 3 + [vmem] + [pl.BlockSpec(memory_space=pltpu.HBM)] * 4 + [vmem] * 6,
            out_specs=vmem,
            scratch_shapes=[
                pltpu.VMEM((shards, half, count), pool.dtype),
                pltpu.VMEM((shards // 2, 2 * half, LANES), jnp.float32),
                pltpu.VMEM((rows, count), jnp.float32),
                pltpu.VMEM(w1.shape, w1.dtype),
                pltpu.VMEM(w2.shape, w2.dtype),
                pltpu.VMEM(w3.shape, w3.dtype),
                pltpu.VMEM(w4.shape, w4.dtype),
                pltpu.SemaphoreType.DMA,
                pltpu.SemaphoreType.DMA((4,)),
            ],
        ),
        compiler_params=pltpu.CompilerParams(vmem_limit_bytes=20 << 20),
        cost_estimate=pl.CostEstimate(flops=flops, bytes_accessed=shards * half * count * 2, transcendentals=0),
        name="score",
    )(positions, pool, codes, piece, scales, w1, w2, w3, w4, b1[None, :], b2[None, :], b3[None, :], b4[None, :], wo, bo[None, :])


def shard_positions(slot_table, shard_total):
    flat = slot_table.reshape(-1)
    matches = flat[None, :] == jnp.arange(shard_total, dtype=jnp.int32)[:, None]
    places = jnp.arange(flat.shape[0], dtype=jnp.int32)[None, :]
    return jnp.sum(jnp.where(matches, places, 0), axis=1)


def exchange_all(codes, scales):
    slot_count, half, samples = codes.shape
    tbl_count = lax.axis_size("tbl")
    count = samples // tbl_count
    values = (codes.astype(jnp.float32) * scales[:, None, :]).astype(codes.dtype)
    packed = values.reshape(slot_count, half, tbl_count, count).transpose(2, 0, 1, 3)
    received = lax.all_to_all(packed, "tbl", split_axis=0, concat_axis=0, tiled=True)
    return received.reshape(tbl_count * slot_count, half, count)


def exchange_line(code, codes, scales, shard_slot):
    nodes, slots = code.nodes, code.slots
    half, samples = codes.shape[1:]
    count = samples // (2 * nodes)
    me = lax.axis_index("tbl").astype(jnp.int32)
    table = plan(shard_slot, me[None], code)
    rounds = table[4, 0]

    def index(place, col):
        return place * 2 + col

    swaps = []
    for side in range(2):
        pairs = [(index(a, c), index(a + 1, c)) for a in range(side, nodes - 1, 2) for c in range(2)]
        swaps.append(pairs + [(b, a) for a, b in pairs])
    across = [(index(a, c), index(a, 1 - c)) for a in range(nodes) for c in range(2)]

    def piece(n, after):
        return lax.ppermute(column_piece(nodes, n, me[None], codes, scales, after, count), "tbl", across)

    def swap(sends):
        return [lax.ppermute(sent, "tbl", pairs) for sent, pairs in zip(sends, swaps)]

    def run(limit, open_end):
        pool, arrived, pieces = None, [], []
        for r in range(limit):
            ready = [p for n, p in enumerate(pieces[:-1]) if PIECE_ROUND[n] <= r]
            recv = arrived[r - LAG] if r >= LAG else None
            pool, *sends = turn(code, table, r, codes, scales, ready, pool, recv, count)
            if r < nodes:
                pieces.append(piece(r, sends[0]))
            arrived.append(swap(sends))
        final, early, late = jnp.int32(limit), arrived[-2], arrived[-1]
        if open_end:
            pool, early, late, pieces = lax.optimization_barrier((pool, early, late, pieces))

            def step(state):
                r, pool, early, late = state
                pool, *sends = turn(code, table, r[None], codes, scales, pieces[:-1], pool, early, count)
                return r + 1, pool, late, swap(sends)

            final, pool, early, late = lax.while_loop(lambda state: state[0] < rounds, step, (final, pool, early, late))
        pool = settle(table, final[None] - 2, pool, early)
        return settle(table, final[None] - 1, pool, late), pieces[-1]

    steps = [functools.partial(run, limit, limit == ROUND_STEPS[-1]) for limit in ROUND_STEPS]
    choice = sum((rounds > limit).astype(jnp.int32) for limit in ROUND_STEPS[:-1])
    pool, piece_own = lax.switch(choice, steps)
    return table, pool, piece_own


def per_device(codes, scales, shard_slot, *parameters):
    layers = tuple(zip(parameters[0::2], parameters[1::2]))
    slots = codes.shape[0]
    tbl_count = lax.axis_size("tbl")
    shards = 2 * TABLES
    if tbl_count % 4 == 0 and slots >= tbl_count:
        code = Codes(tbl_count // 2, slots)
        places, pool, piece = exchange_line(code, codes, scales, shard_slot)
        limits = (slots, code.piece, code.pool, 5)
    else:
        pool = exchange_all(codes, scales)
        piece, places, limits = pool, shard_positions(shard_slot, shards)[None, :], (slots, 0, 0, 0)
    logits = score(pool, codes, piece, scales, places, shards, limits, layers)
    return lax.all_gather(logits, "pair", axis=0, tiled=True)


def solution(mesh):
    return jax.shard_map(
        per_device,
        mesh=mesh,
        in_specs=(P("tbl", None, "pair"), P("tbl", "pair")) + (P(),) * 11,
        out_specs=P(None, "tbl"),
        check_vma=False,
    )
```

```python
import functools
import jax
import jax.numpy as jnp
from jax import lax
from jax.experimental import pallas as pl
from jax.experimental.pallas import tpu as pltpu
from jax.sharding import PartitionSpec as P

TABLES = 27
LANES = 128
CHUNK = 6
ROUND_STEPS = (12, 13, 15)
LAG = 2
PIECE_AFTER = (0, 2, 4, 6)
PIECE_ROUND = (3, 5, 7, 10)
SPAN = 256


def piece_order(nodes, node):
    if node < nodes // 2:
        return tuple(range(nodes - 1, node, -1)) + tuple(range(node)) + (node,)
    return tuple(range(node)) + tuple(range(nodes - 1, node, -1)) + (node,)


def whole_chunks(value):
    return (value * (-(-65536 // CHUNK))) >> 16


class Codes:
    def __init__(self, nodes, slots):
        self.nodes, self.slots = nodes, slots
        self.piece = 2 * nodes * slots
        self.pool = self.piece + nodes * slots
        self.units = nodes * nodes * slots
        self.stage = self.pool + self.units
        self.pool_rows = self.units + 2 * CHUNK


def time_lists(code, counts, column, ends):
    nodes, slots = code.nodes, code.slots
    half = nodes // 2
    rows = {}
    for place in range(nodes):
        for other in range(2):
            row = column if other == 0 else 1 - column
            count = jnp.where(row == 0, counts[2 * place], counts[2 * place + 1])
            first = 0 if place < half else slots - count
            rows[place, other] = (count, first, ((place % half) * 2 + row) * slots)

    lists = {}
    for up in (True, False):
        starts = {}
        path = range(nodes - 1) if up else range(nodes - 1, 0, -1)
        for place in path:
            goals = range(nodes - 1, place, -1) if up else range(place)
            before = range(place - 1, -1, -1) if up else range(place + 1, nodes)
            pieces = piece_order(nodes, place)
            items = [(source, other, goal) for other in range(2) for goal in goals for source in (place, *before)]
            end, here, segments = jnp.int32(0), {}, []
            for source, other, goal in items:
                count, first, _ = rows[source, other]
                if source != place:
                    ready = starts[source, other, goal] + LAG * CHUNK
                elif other:
                    ready = jnp.int32(PIECE_ROUND[pieces.index(goal)] * CHUNK)
                else:
                    ready = jnp.int32(0)
                start = jnp.maximum(end, ready)
                segments.append((source, other, goal, start, starts.get((source, other, goal))))
                here[source, other, goal] = start
                end = jnp.where(count > 0, start + count, end)
            lists[up, place] = segments
            ends.append(end)
            starts = here
    return rows, lists


def plan_kernel(code, slot_ref, me_ref, out_ref):
    nodes, slots = code.nodes, code.slots
    me = me_ref[0]
    column, node = me & 1, me >> 1
    counts = []
    for row in range(2 * nodes):
        total = jnp.int32(0)
        for slot in range(slots):
            total += (slot_ref[row, slot] >= 0).astype(jnp.int32)
        counts.append(total)
    ends = []
    for flip in range(2):
        rows, lists = time_lists(code, counts, column ^ flip, ends)
        if flip == 0:
            own_rows, own_lists = rows, lists
    rows, lists = own_rows, own_lists
    last = functools.reduce(jnp.maximum, ends)

    spot = lax.broadcasted_iota(jnp.int32, (1, SPAN), 1)
    turn_of = whole_chunks(spot)
    rest = spot - turn_of * CHUNK
    tables = {}
    for (up, place), segments in lists.items():
        side = place % 2 if up else (place - 1) % 2
        came = 1 - side
        send = jnp.zeros((1, SPAN), jnp.int32)
        unit = code.units + side * CHUNK + rest
        for source, other, goal, start, earlier in segments:
            count, first, base = rows[source, other]
            index = spot - start
            inside = (index >= 0) & (index < count)
            slot = first + index
            this = goal * nodes * slots + base + slot
            if source != place:
                arrived = earlier + index
                came_in = whole_chunks(arrived)
                staged = code.stage + came * CHUNK + arrived - came_in * CHUNK
                origin = jnp.where(turn_of - came_in == LAG, staged, code.pool + this)
            elif other:
                origin = code.piece + piece_order(nodes, place).index(goal) * slots + slot
            else:
                origin = (goal * 2 + column) * slots + slot
            send = jnp.where(inside, origin, send)
            unit = jnp.where(inside, this, unit)
        tables[up, place] = (send, unit)
    blank = jnp.zeros((1, SPAN), jnp.int32)
    for side in range(2):
        sent = blank
        kept = code.units + side * CHUNK + rest
        for place in range(nodes):
            up = place % 2 == side
            peer = place + 1 if up else place - 1
            if 0 <= peer < nodes:
                sent = jnp.where(node == place, tables[up, place][0], sent)
                kept = jnp.where(node == place, tables[not up, peer][1], kept)
        out_ref[side:side + 1, :] = sent
        out_ref[2 + side:3 + side, :] = kept
    out_ref[4:5, :] = blank + lax.div(last + CHUNK - 1, jnp.int32(CHUNK))
    places = blank
    for row in range(2 * nodes):
        base = code.pool + (node * nodes + row % nodes) * slots
        base = jnp.where(row == (me ^ 1), code.piece, base)
        base = jnp.where(row == me, me * slots, base)
        for slot in range(slots):
            places = jnp.where(spot == slot_ref[row, slot], base + slot, places)
    out_ref[5:6, :] = places
    out_ref[6:8, :] = jnp.zeros((2, SPAN), jnp.int32)


def plan(shard_slot, me, code):
    return pl.pallas_call(
        functools.partial(plan_kernel, code),
        out_shape=jax.ShapeDtypeStruct((8, SPAN), jnp.int32),
        in_specs=[pl.BlockSpec(memory_space=pltpu.SMEM)] * 2,
        out_specs=pl.BlockSpec(memory_space=pltpu.VMEM),
        name="plan",
    )(shard_slot, me)


def rescale(block, scales_ref, slot, start, count):
    factor = scales_ref[pl.ds(slot, 1), pl.ds(pl.multiple_of(start, LANES), count)]
    return (block.astype(jnp.float32) * factor).astype(block.dtype)


def turn_kernel(code, n_pieces, has_pool, has_recv, base, table_ref, *refs):
    refs = list(refs)
    if base is None:
        base = refs.pop(0)[0] * CHUNK
    codes_ref, scales_ref = refs.pop(0), refs.pop(0)
    pieces = [refs.pop(0) for _ in range(n_pieces)]
    if has_pool:
        refs.pop(0)
    recvs = [refs.pop(0) for _ in range(2)] if has_recv else []
    pool_ref, send_a, send_b, buf, load_sem, recv_sem, pool_sem = refs
    slots = code.slots
    count = buf.shape[2]
    loads = [pltpu.make_async_copy(ref, buf.at[pl.ds(s * CHUNK, CHUNK)], recv_sem.at[s]) for s, ref in enumerate(recvs)]

    def gather(side, send, c, carry):
        e = table_ref[side, base + c]
        goal = send.at[c]

        @pl.when(e < code.piece)
        def _():
            dest = lax.div(e, jnp.int32(slots))
            lanes = pl.ds(pl.multiple_of(dest * count, count), count)
            pltpu.make_async_copy(codes_ref.at[e - dest * slots, :, lanes], goal, load_sem).start()

        if has_recv:
            @pl.when(e >= code.piece)
            def _():
                for n, piece in enumerate(pieces):
                    low = code.piece + n * slots

                    @pl.when((e >= low) & (e < low + slots))
                    def _():
                        pltpu.make_async_copy(piece.at[e - low], goal, load_sem).start()

                @pl.when((e >= code.pool) & (e < code.stage))
                def _():
                    pltpu.make_async_copy(pool_ref.at[e - code.pool], goal, load_sem).start()

                for n, recv in enumerate(recvs):
                    low = code.stage + n * CHUNK

                    @pl.when((e >= low) & (e < low + CHUNK))
                    def _():
                        pltpu.make_async_copy(recv.at[e - low], goal, load_sem).start()

        return carry

    def gathered(send, c, carry):
        pltpu.make_async_copy(codes_ref.at[0, :, pl.ds(0, count)], send.at[c], load_sem).wait()
        return carry

    def keep(side, c, carry):
        row = table_ref[2 + side, base - LAG * CHUNK + c]
        pltpu.make_async_copy(buf.at[side * CHUNK + c], pool_ref.at[row], pool_sem).start()
        return carry

    def kept(c, carry):
        pltpu.make_async_copy(buf.at[0], pool_ref.at[0], pool_sem).wait()
        return carry

    def scale(side, send, c, carry):
        e = table_ref[side, base + c]

        @pl.when(e < code.piece)
        def _():
            dest = lax.div(e, jnp.int32(slots))
            send[c] = rescale(send[c], scales_ref, e - dest * slots, dest * count, count)

        return carry

    sides = ((0, send_a), (1, send_b))
    for side, send in sides:
        lax.fori_loop(0, CHUNK, functools.partial(gather, side, send), 0)
    for copy in loads:
        copy.start()
    for side, send in sides:
        lax.fori_loop(0, CHUNK, functools.partial(gathered, send), 0)
    if has_recv:
        for side in range(2):
            loads[side].wait()
            lax.fori_loop(0, CHUNK, functools.partial(keep, side), 0)
    for side, send in sides:
        lax.fori_loop(0, CHUNK, functools.partial(scale, side, send), 0)
    if has_recv:
        lax.fori_loop(0, 2 * CHUNK, kept, 0)


def turn(code, table, number, codes, scales, pieces, pool, recv, count):
    half = codes.shape[1]
    anywhere = pl.BlockSpec(memory_space=pl.ANY)
    vmem = pl.BlockSpec(memory_space=pltpu.VMEM)
    block = jax.ShapeDtypeStruct((CHUNK, half, count), codes.dtype)
    operands = [codes, scales, *pieces] + ([] if pool is None else [pool]) + list(recv or ())
    specs = [anywhere, vmem] + [anywhere] * (len(operands) - 2)
    fixed = isinstance(number, int)
    scalars = (table,) if fixed else (table, number)
    aliases = {} if pool is None else {len(scalars) + 2 + len(pieces): 0}
    size = CHUNK * half * count * 2
    base = number * CHUNK if fixed else None
    return pl.pallas_call(
        functools.partial(turn_kernel, code, len(pieces), pool is not None, recv is not None, base),
        out_shape=(jax.ShapeDtypeStruct((code.pool_rows, half, count), codes.dtype), block, block),
        grid_spec=pltpu.PrefetchScalarGridSpec(
            num_scalar_prefetch=len(scalars),
            grid=(),
            in_specs=specs,
            out_specs=(anywhere, vmem, vmem),
            scratch_shapes=[
                pltpu.VMEM((2 * CHUNK, half, count), codes.dtype),
                pltpu.SemaphoreType.DMA,
                pltpu.SemaphoreType.DMA((2,)),
                pltpu.SemaphoreType.DMA,
            ],
        ),
        input_output_aliases=aliases,
        compiler_params=pltpu.CompilerParams(vmem_limit_bytes=8 << 20),
        cost_estimate=pl.CostEstimate(flops=size, bytes_accessed=8 * size, transcendentals=0),
        name="turn",
    )(*scalars, *operands)


def piece_kernel(nodes, n, me_ref, codes_ref, scales_ref, after_ref, out_ref, sem):
    me = me_ref[0]
    goal = jnp.int32(0)
    for place in range(nodes):
        goal = jnp.where((me >> 1) == place, piece_order(nodes, place)[n], goal)
    slots, _, count = out_ref.shape
    start = pl.multiple_of((goal * 2 + 1 - (me & 1)) * count, count)
    copy = pltpu.make_async_copy(codes_ref.at[:, :, pl.ds(start, count)], out_ref, sem)
    copy.start()
    copy.wait()

    def scale(slot, carry):
        out_ref[slot] = rescale(out_ref[slot], scales_ref, slot, start, count)
        return carry

    lax.fori_loop(0, slots, scale, 0)


def column_piece(nodes, n, me, codes, scales, after, count):
    slots, half, _ = codes.shape
    anywhere = pl.BlockSpec(memory_space=pl.ANY)
    vmem = pl.BlockSpec(memory_space=pltpu.VMEM)
    return pl.pallas_call(
        functools.partial(piece_kernel, nodes, n),
        out_shape=jax.ShapeDtypeStruct((slots, half, count), codes.dtype),
        grid_spec=pltpu.PrefetchScalarGridSpec(
            num_scalar_prefetch=1,
            grid=(),
            in_specs=[anywhere, vmem, anywhere],
            out_specs=vmem,
            scratch_shapes=[pltpu.SemaphoreType.DMA],
        ),
        compiler_params=pltpu.CompilerParams(vmem_limit_bytes=8 << 20),
        cost_estimate=pl.CostEstimate(flops=slots * half * count, bytes_accessed=4 * slots * half * count, transcendentals=0),
        name="piece",
    )(me, codes, scales, after)


def settle_kernel(table_ref, round_ref, pool_in, recv_a, recv_b, pool_ref, buf, load_sem, pool_sem):
    base = round_ref[0] * CHUNK
    loads = [pltpu.make_async_copy(ref, buf.at[pl.ds(n * CHUNK, CHUNK)], load_sem.at[n]) for n, ref in enumerate((recv_a, recv_b))]
    for copy in loads:
        copy.start()
    stores = []
    for n in range(2):
        loads[n].wait()
        for c in range(CHUNK):
            row = table_ref[2 + n, base + c]
            stores.append(pltpu.make_async_copy(buf.at[n * CHUNK + c], pool_ref.at[row], pool_sem))
            stores[-1].start()
    for copy in stores:
        copy.wait()


def settle(table, number, pool, recv):
    anywhere = pl.BlockSpec(memory_space=pl.ANY)
    return pl.pallas_call(
        settle_kernel,
        out_shape=jax.ShapeDtypeStruct(pool.shape, pool.dtype),
        grid_spec=pltpu.PrefetchScalarGridSpec(
            num_scalar_prefetch=2,
            grid=(),
            in_specs=[anywhere] * 3,
            out_specs=anywhere,
            scratch_shapes=[
                pltpu.VMEM((2 * CHUNK,) + pool.shape[1:], pool.dtype),
                pltpu.SemaphoreType.DMA((2,)),
                pltpu.SemaphoreType.DMA,
            ],
        ),
        input_output_aliases={2: 0},
        compiler_params=pltpu.CompilerParams(vmem_limit_bytes=8 << 20),
        name="settle",
    )(table, number, pool, *recv)


def score_kernel(limits, pos_ref, pool_ref, codes_ref, piece_ref, scales_ref, *refs):
    sources, refs = refs[:9], refs[9:]
    bo_ref, out_ref, picked, wide, inter = refs[:5]
    copies, (pick_sem, weight_sem) = refs[5:14], refs[14:]
    w1, w2, w3, w4, b1_ref, b2_ref, b3_ref, b4_ref, wo_ref = copies
    shards, half, count = picked.shape
    tables = shards // 2
    weights = [pltpu.make_async_copy(src, dst, weight_sem.at[n]) for n, (src, dst) in enumerate(zip(sources, copies))]

    slots, piece_base, pool_base, table_row = limits

    def begin(shard, carry):
        e = pos_ref[table_row, shard]
        dest = lax.div(e, jnp.int32(slots))

        @pl.when(e < piece_base)
        def _():
            lanes = pl.ds(pl.multiple_of(dest * count, count), count)
            pltpu.make_async_copy(codes_ref.at[e - dest * slots, :, lanes], picked.at[shard], pick_sem).start()

        @pl.when((e >= piece_base) & (e < pool_base))
        def _():
            pltpu.make_async_copy(piece_ref.at[e - piece_base], picked.at[shard], pick_sem).start()

        @pl.when(e >= pool_base)
        def _():
            pltpu.make_async_copy(pool_ref.at[e - pool_base], picked.at[shard], pick_sem).start()

        return carry

    def finish(shard, carry):
        pltpu.make_async_copy(pool_ref.at[0], picked.at[shard], pick_sem).wait()
        return carry

    def rescale(shard, carry):
        e = pos_ref[table_row, shard]
        dest = lax.div(e, jnp.int32(slots))

        @pl.when(e < piece_base)
        def _():
            lanes = pl.ds(pl.multiple_of(dest * count, count), count)
            factor = scales_ref[pl.ds(e - dest * slots, 1), lanes]
            picked[shard] = (picked[shard].astype(jnp.float32) * factor).astype(picked.dtype)

        return carry

    lax.fori_loop(0, shards, begin, 0)
    for copy in weights:
        copy.start()
    lax.fori_loop(0, shards, finish, 0)
    lax.fori_loop(0, shards, rescale, 0)

    def gram_block(block, carry):
        lanes = pl.ds(pl.multiple_of(block * LANES, LANES), LANES)
        for shard in range(shards):
            wide[shard // 2, (shard % 2) * half:(shard % 2 + 1) * half, :] = picked[shard, :, lanes].astype(jnp.float32)
        row = 0
        for i in range(tables):
            left = wide[i]
            for j in range(i + 1, tables):
                inter[row:row + 1, lanes] = jnp.sum(left * wide[j], axis=0, keepdims=True)
                row += 1
        return carry

    lax.fori_loop(0, count // LANES, gram_block, 0)
    for copy in weights:
        copy.wait()
    step = 2 * LANES if count % (2 * LANES) == 0 else LANES

    def dense(hidden, weight, bias):
        product = jnp.dot(hidden, weight[...], preferred_element_type=jnp.float32)
        return jnp.maximum(product + bias[...], 0.0).astype(jnp.bfloat16)

    def top_block(block, carry):
        lanes = pl.ds(pl.multiple_of(block * step, step), step)
        hidden = jnp.transpose(inter[:, lanes]).astype(jnp.bfloat16)
        hidden = dense(hidden, w1, b1_ref)
        hidden = dense(hidden, w2, b2_ref)
        hidden = dense(hidden, w3, b3_ref)
        hidden = dense(hidden, w4, b4_ref)
        final = lax.dot_general(wo_ref[...], hidden, (((1,), (1,)), ((), ())), preferred_element_type=jnp.float32)
        out_ref[:, lanes] = final[0:1] + bo_ref[0]
        return carry

    lax.fori_loop(0, count // step, top_block, 0)


def score(pool, codes, piece, scales, positions, shards, limits, layers):
    (w1, b1), (w2, b2), (w3, b3), (w4, b4), (wo, bo) = layers
    half, count = pool.shape[1:]
    rows = w1.shape[0]
    wo = wo[None, :]
    anywhere = pl.BlockSpec(memory_space=pl.ANY)
    vmem = pl.BlockSpec(memory_space=pltpu.VMEM)
    flops = 2 * count * sum(w.size for w in (w1, w2, w3, w4))
    parts = (w1, w2, w3, w4, b1[None, :], b2[None, :], b3[None, :], b4[None, :], wo)
    return pl.pallas_call(
        functools.partial(score_kernel, limits),
        out_shape=jax.ShapeDtypeStruct((1, count), jnp.float32),
        grid_spec=pltpu.PrefetchScalarGridSpec(
            num_scalar_prefetch=1,
            grid=(),
            in_specs=[anywhere] * 3 + [vmem] + [pl.BlockSpec(memory_space=pltpu.HBM)] * 9 + [pl.BlockSpec(memory_space=pltpu.SMEM)],
            out_specs=vmem,
            scratch_shapes=[
                pltpu.VMEM((shards, half, count), pool.dtype),
                pltpu.VMEM((shards // 2, 2 * half, LANES), jnp.float32),
                pltpu.VMEM((rows, count), jnp.float32),
                *(pltpu.VMEM(part.shape, part.dtype) for part in parts),
                pltpu.SemaphoreType.DMA,
                pltpu.SemaphoreType.DMA((len(parts),)),
            ],
        ),
        compiler_params=pltpu.CompilerParams(vmem_limit_bytes=20 << 20),
        cost_estimate=pl.CostEstimate(flops=flops, bytes_accessed=shards * half * count * 2, transcendentals=0),
        name="score",
    )(positions, pool, codes, piece, scales, *parts, bo)


def shard_positions(slot_table, shard_total):
    flat = slot_table.reshape(-1)
    matches = flat[None, :] == jnp.arange(shard_total, dtype=jnp.int32)[:, None]
    places = jnp.arange(flat.shape[0], dtype=jnp.int32)[None, :]
    return jnp.sum(jnp.where(matches, places, 0), axis=1)


def exchange_all(codes, scales):
    slot_count, half, samples = codes.shape
    tbl_count = lax.axis_size("tbl")
    count = samples // tbl_count
    values = (codes.astype(jnp.float32) * scales[:, None, :]).astype(codes.dtype)
    packed = values.reshape(slot_count, half, tbl_count, count).transpose(2, 0, 1, 3)
    received = lax.all_to_all(packed, "tbl", split_axis=0, concat_axis=0, tiled=True)
    return received.reshape(tbl_count * slot_count, half, count)


def exchange_line(code, codes, scales, shard_slot):
    nodes = code.nodes
    _, samples = codes.shape[1:]
    count = samples // (2 * nodes)
    me = lax.axis_index("tbl").astype(jnp.int32)
    table = plan(shard_slot, me[None], code)
    rounds = table[4, 0]

    def index(place, col):
        return place * 2 + col

    swaps = []
    for side in range(2):
        pairs = [(index(a, c), index(a + 1, c)) for a in range(side, nodes - 1, 2) for c in range(2)]
        swaps.append(pairs + [(b, a) for a, b in pairs])
    across = [(index(a, c), index(a, 1 - c)) for a in range(nodes) for c in range(2)]

    def piece(n, after):
        part = column_piece(nodes, n, me[None], codes, scales, after, count)
        return lax.ppermute(part, "tbl", across)

    def swap(sends):
        swapped = []
        for sent, pairs in zip(sends, swaps):
            swapped.append(lax.ppermute(sent, "tbl", pairs))
        return swapped

    def run(limit, open_end):
        return rounds_of(limit, open_end)

    def rounds_of(limit, open_end):
        pool, arrived, pieces = None, [], [piece(0, scales)]
        for r in range(limit):
            ready = [p for n, p in enumerate(pieces[:nodes - 1]) if PIECE_ROUND[n] <= r]
            recv = arrived[r - LAG] if r >= LAG else None
            pool, *sends = turn(code, table, r, codes, scales, ready, pool, recv, count)
            arrived.append(swap(sends))
            if r in PIECE_AFTER[1:]:
                pieces.append(piece(len(pieces), sends[0]))
        final, early, late = jnp.int32(limit), arrived[-2], arrived[-1]
        if open_end:
            pool, early, late, pieces = lax.optimization_barrier((pool, early, late, pieces))

            def step(state):
                r, pool, early, late = state
                pool, *sends = turn(code, table, r[None], codes, scales, pieces[:-1], pool, early, count)
                return r + 1, pool, late, swap(sends)

            final, pool, early, late = lax.while_loop(lambda state: state[0] < rounds, step, (final, pool, early, late))
        pool = settle(table, final[None] - 2, pool, early)
        return settle(table, final[None] - 1, pool, late), pieces[-1]

    steps = [functools.partial(run, limit, limit == ROUND_STEPS[-1]) for limit in ROUND_STEPS]
    choice = sum((rounds > limit).astype(jnp.int32) for limit in ROUND_STEPS[:-1])
    pool, piece_own = lax.switch(choice, steps)
    return table, pool, piece_own


def per_device(codes, scales, shard_slot, *parameters):
    layers = tuple(zip(parameters[0::2], parameters[1::2]))
    slots = codes.shape[0]
    tbl_count = lax.axis_size("tbl")
    shards = 2 * TABLES
    if tbl_count % 4 == 0 and slots >= tbl_count:
        code = Codes(tbl_count // 2, slots)
        places, pool, piece = exchange_line(code, codes, scales, shard_slot)
        limits = (slots, code.piece, code.pool, 5)
    else:
        pool = exchange_all(codes, scales)
        piece, places, limits = pool, shard_positions(shard_slot, shards)[None, :], (slots, 0, 0, 0)
    logits = score(pool, codes, piece, scales, places, shards, limits, layers)
    return lax.all_gather(logits, "pair", axis=0, tiled=True)


def solution(mesh):
    return jax.shard_map(
        per_device,
        mesh=mesh,
        in_specs=(P("tbl", None, "pair"), P("tbl", "pair")) + (P(),) * 11,
        out_specs=P(None, "tbl"),
        check_vma=False,
    )
```

```python
import functools
import jax
import jax.numpy as jnp
from jax import lax
from jax.experimental import pallas as pl
from jax.experimental.pallas import tpu as pltpu
from jax.sharding import PartitionSpec as P

TABLES = 27
LANES = 128
CHUNK = 6
ROUND_STEPS = (12, 13, 15)
LAG = 2
PIECE_AFTER = (0, 2, 4, 6)
PIECE_ROUND = (3, 5, 7, 10)
SPAN = 256


def piece_order(nodes, node):
    if node < nodes // 2:
        return tuple(range(nodes - 1, node, -1)) + tuple(range(node)) + (node,)
    return tuple(range(node)) + tuple(range(nodes - 1, node, -1)) + (node,)


def whole_chunks(value):
    return (value * (-(-65536 // CHUNK))) >> 16


class Codes:
    def __init__(self, nodes, slots):
        self.nodes, self.slots = nodes, slots
        self.piece = 2 * nodes * slots
        self.pool = self.piece + nodes * slots
        self.units = nodes * nodes * slots
        self.stage = self.pool + self.units
        self.pool_rows = self.units + 2 * CHUNK


def time_lists(code, counts, column, ends):
    nodes, slots = code.nodes, code.slots
    half = nodes // 2
    rows = {}
    for place in range(nodes):
        for other in range(2):
            row = column if other == 0 else 1 - column
            count = jnp.where(row == 0, counts[2 * place], counts[2 * place + 1])
            first = 0 if place < half else slots - count
            rows[place, other] = (count, first, ((place % half) * 2 + row) * slots)

    lists = {}
    for up in (True, False):
        starts = {}
        path = range(nodes - 1) if up else range(nodes - 1, 0, -1)
        for place in path:
            goals = range(nodes - 1, place, -1) if up else range(place)
            before = range(place - 1, -1, -1) if up else range(place + 1, nodes)
            pieces = piece_order(nodes, place)
            items = [(source, other, goal) for other in range(2) for goal in goals for source in (place, *before)]
            if not before:
                items.insert(len(goals) - 1, items.pop(len(goals)))
            end, here, segments = jnp.int32(0), {}, []
            for source, other, goal in items:
                count, first, _ = rows[source, other]
                if source != place:
                    ready = starts[source, other, goal] + LAG * CHUNK
                elif other:
                    ready = jnp.int32(PIECE_ROUND[pieces.index(goal)] * CHUNK)
                else:
                    ready = jnp.int32(0)
                start = jnp.maximum(end, ready)
                segments.append((source, other, goal, start, starts.get((source, other, goal))))
                here[source, other, goal] = start
                end = jnp.where(count > 0, start + count, end)
            lists[up, place] = segments
            ends.append(end)
            starts = here
    return rows, lists


def plan_kernel(code, slot_ref, me_ref, out_ref):
    nodes, slots = code.nodes, code.slots
    me = me_ref[0]
    column, node = me & 1, me >> 1
    counts = []
    for row in range(2 * nodes):
        total = jnp.int32(0)
        for slot in range(slots):
            total += (slot_ref[row, slot] >= 0).astype(jnp.int32)
        counts.append(total)
    ends = []
    for flip in range(2):
        rows, lists = time_lists(code, counts, column ^ flip, ends)
        if flip == 0:
            own_rows, own_lists = rows, lists
    rows, lists = own_rows, own_lists
    last = functools.reduce(jnp.maximum, ends)

    spot = lax.broadcasted_iota(jnp.int32, (1, SPAN), 1)
    turn_of = whole_chunks(spot)
    rest = spot - turn_of * CHUNK
    tables = {}
    for (up, place), segments in lists.items():
        side = place % 2 if up else (place - 1) % 2
        came = 1 - side
        send = jnp.zeros((1, SPAN), jnp.int32)
        unit = code.units + side * CHUNK + rest
        for source, other, goal, start, earlier in segments:
            count, first, base = rows[source, other]
            index = spot - start
            inside = (index >= 0) & (index < count)
            slot = first + index
            this = goal * nodes * slots + base + slot
            if source != place:
                arrived = earlier + index
                came_in = whole_chunks(arrived)
                staged = code.stage + came * CHUNK + arrived - came_in * CHUNK
                origin = jnp.where(turn_of - came_in == LAG, staged, code.pool + this)
            elif other:
                origin = code.piece + piece_order(nodes, place).index(goal) * slots + slot
            else:
                origin = (goal * 2 + column) * slots + slot
            send = jnp.where(inside, origin, send)
            unit = jnp.where(inside, this, unit)
        tables[up, place] = (send, unit)
    blank = jnp.zeros((1, SPAN), jnp.int32)
    for side in range(2):
        sent = blank
        kept = code.units + side * CHUNK + rest
        for place in range(nodes):
            up = place % 2 == side
            peer = place + 1 if up else place - 1
            if 0 <= peer < nodes:
                sent = jnp.where(node == place, tables[up, place][0], sent)
                kept = jnp.where(node == place, tables[not up, peer][1], kept)
        out_ref[side:side + 1, :] = sent
        out_ref[2 + side:3 + side, :] = kept
    out_ref[4:5, :] = blank + lax.div(last + CHUNK - 1, jnp.int32(CHUNK))
    places = blank
    for row in range(2 * nodes):
        base = code.pool + (node * nodes + row % nodes) * slots
        base = jnp.where(row == (me ^ 1), code.piece, base)
        base = jnp.where(row == me, me * slots, base)
        for slot in range(slots):
            places = jnp.where(spot == slot_ref[row, slot], base + slot, places)
    out_ref[5:6, :] = places
    out_ref[6:8, :] = jnp.zeros((2, SPAN), jnp.int32)


def plan(shard_slot, me, code):
    return pl.pallas_call(
        functools.partial(plan_kernel, code),
        out_shape=jax.ShapeDtypeStruct((8, SPAN), jnp.int32),
        in_specs=[pl.BlockSpec(memory_space=pltpu.SMEM)] * 2,
        out_specs=pl.BlockSpec(memory_space=pltpu.VMEM),
        name="plan",
    )(shard_slot, me)


def rescale(block, scales_ref, slot, start, count):
    factor = scales_ref[pl.ds(slot, 1), pl.ds(pl.multiple_of(start, LANES), count)]
    return (block.astype(jnp.float32) * factor).astype(block.dtype)


def turn_kernel(code, n_pieces, has_pool, has_recv, base, table_ref, *refs):
    refs = list(refs)
    if base is None:
        base = refs.pop(0)[0] * CHUNK
    codes_ref, scales_ref = refs.pop(0), refs.pop(0)
    pieces = [refs.pop(0) for _ in range(n_pieces)]
    if has_pool:
        refs.pop(0)
    recvs = [refs.pop(0) for _ in range(2)] if has_recv else []
    pool_ref, send_a, send_b, buf, load_sem, recv_sem, pool_sem = refs
    slots = code.slots
    count = buf.shape[2]
    loads = [pltpu.make_async_copy(ref, buf.at[pl.ds(s * CHUNK, CHUNK)], recv_sem.at[s]) for s, ref in enumerate(recvs)]

    def gather(side, send, c, carry):
        e = table_ref[side, base + c]
        goal = send.at[c]

        @pl.when(e < code.piece)
        def _():
            dest = lax.div(e, jnp.int32(slots))
            lanes = pl.ds(pl.multiple_of(dest * count, count), count)
            pltpu.make_async_copy(codes_ref.at[e - dest * slots, :, lanes], goal, load_sem).start()

        if has_recv:
            @pl.when(e >= code.piece)
            def _():
                for n, piece in enumerate(pieces):
                    low = code.piece + n * slots

                    @pl.when((e >= low) & (e < low + slots))
                    def _():
                        pltpu.make_async_copy(piece.at[e - low], goal, load_sem).start()

                @pl.when((e >= code.pool) & (e < code.stage))
                def _():
                    pltpu.make_async_copy(pool_ref.at[e - code.pool], goal, load_sem).start()

                for n, recv in enumerate(recvs):
                    low = code.stage + n * CHUNK

                    @pl.when((e >= low) & (e < low + CHUNK))
                    def _():
                        pltpu.make_async_copy(recv.at[e - low], goal, load_sem).start()

        return carry

    def gathered(send, c, carry):
        pltpu.make_async_copy(codes_ref.at[0, :, pl.ds(0, count)], send.at[c], load_sem).wait()
        return carry

    def keep(side, c, carry):
        row = table_ref[2 + side, base - LAG * CHUNK + c]
        pltpu.make_async_copy(buf.at[side * CHUNK + c], pool_ref.at[row], pool_sem).start()
        return carry

    def kept(c, carry):
        pltpu.make_async_copy(buf.at[0], pool_ref.at[0], pool_sem).wait()
        return carry

    def scale(side, send, c, carry):
        e = table_ref[side, base + c]

        @pl.when(e < code.piece)
        def _():
            dest = lax.div(e, jnp.int32(slots))
            send[c] = rescale(send[c], scales_ref, e - dest * slots, dest * count, count)

        return carry

    sides = ((0, send_a), (1, send_b))
    for side, send in sides:
        lax.fori_loop(0, CHUNK, functools.partial(gather, side, send), 0)
    for copy in loads:
        copy.start()
    for side, send in sides:
        lax.fori_loop(0, CHUNK, functools.partial(gathered, send), 0)
    if has_recv:
        for side in range(2):
            loads[side].wait()
            lax.fori_loop(0, CHUNK, functools.partial(keep, side), 0)
    for side, send in sides:
        lax.fori_loop(0, CHUNK, functools.partial(scale, side, send), 0)
    if has_recv:
        lax.fori_loop(0, 2 * CHUNK, kept, 0)


def turn(code, table, number, codes, scales, pieces, pool, recv, count):
    half = codes.shape[1]
    anywhere = pl.BlockSpec(memory_space=pl.ANY)
    vmem = pl.BlockSpec(memory_space=pltpu.VMEM)
    block = jax.ShapeDtypeStruct((CHUNK, half, count), codes.dtype)
    operands = [codes, scales, *pieces] + ([] if pool is None else [pool]) + list(recv or ())
    specs = [anywhere, vmem] + [anywhere] * (len(operands) - 2)
    fixed = isinstance(number, int)
    scalars = (table,) if fixed else (table, number)
    aliases = {} if pool is None else {len(scalars) + 2 + len(pieces): 0}
    size = CHUNK * half * count * 2
    base = number * CHUNK if fixed else None
    return pl.pallas_call(
        functools.partial(turn_kernel, code, len(pieces), pool is not None, recv is not None, base),
        out_shape=(jax.ShapeDtypeStruct((code.pool_rows, half, count), codes.dtype), block, block),
        grid_spec=pltpu.PrefetchScalarGridSpec(
            num_scalar_prefetch=len(scalars),
            grid=(),
            in_specs=specs,
            out_specs=(anywhere, vmem, vmem),
            scratch_shapes=[
                pltpu.VMEM((2 * CHUNK, half, count), codes.dtype),
                pltpu.SemaphoreType.DMA,
                pltpu.SemaphoreType.DMA((2,)),
                pltpu.SemaphoreType.DMA,
            ],
        ),
        input_output_aliases=aliases,
        compiler_params=pltpu.CompilerParams(vmem_limit_bytes=8 << 20),
        cost_estimate=pl.CostEstimate(flops=size, bytes_accessed=8 * size, transcendentals=0),
        name="turn",
    )(*scalars, *operands)


def piece_kernel(nodes, n, me_ref, codes_ref, scales_ref, after_ref, out_ref, sem):
    me = me_ref[0]
    goal = jnp.int32(0)
    for place in range(nodes):
        goal = jnp.where((me >> 1) == place, piece_order(nodes, place)[n], goal)
    slots, _, count = out_ref.shape
    start = pl.multiple_of((goal * 2 + 1 - (me & 1)) * count, count)
    copy = pltpu.make_async_copy(codes_ref.at[:, :, pl.ds(start, count)], out_ref, sem)
    copy.start()
    copy.wait()

    def scale(slot, carry):
        out_ref[slot] = rescale(out_ref[slot], scales_ref, slot, start, count)
        return carry

    lax.fori_loop(0, slots, scale, 0)


def column_piece(nodes, n, me, codes, scales, after, count):
    slots, half, _ = codes.shape
    anywhere = pl.BlockSpec(memory_space=pl.ANY)
    vmem = pl.BlockSpec(memory_space=pltpu.VMEM)
    return pl.pallas_call(
        functools.partial(piece_kernel, nodes, n),
        out_shape=jax.ShapeDtypeStruct((slots, half, count), codes.dtype),
        grid_spec=pltpu.PrefetchScalarGridSpec(
            num_scalar_prefetch=1,
            grid=(),
            in_specs=[anywhere, vmem, anywhere],
            out_specs=vmem,
            scratch_shapes=[pltpu.SemaphoreType.DMA],
        ),
        compiler_params=pltpu.CompilerParams(vmem_limit_bytes=8 << 20),
        cost_estimate=pl.CostEstimate(flops=slots * half * count, bytes_accessed=4 * slots * half * count, transcendentals=0),
        name="piece",
    )(me, codes, scales, after)


def settle_kernel(table_ref, round_ref, pool_in, recv_a, recv_b, pool_ref, buf, load_sem, pool_sem):
    base = round_ref[0] * CHUNK
    loads = [pltpu.make_async_copy(ref, buf.at[pl.ds(n * CHUNK, CHUNK)], load_sem.at[n]) for n, ref in enumerate((recv_a, recv_b))]
    for copy in loads:
        copy.start()
    stores = []
    for n in range(2):
        loads[n].wait()
        for c in range(CHUNK):
            row = table_ref[2 + n, base + c]
            stores.append(pltpu.make_async_copy(buf.at[n * CHUNK + c], pool_ref.at[row], pool_sem))
            stores[-1].start()
    for copy in stores:
        copy.wait()


def settle(table, number, pool, recv):
    anywhere = pl.BlockSpec(memory_space=pl.ANY)
    return pl.pallas_call(
        settle_kernel,
        out_shape=jax.ShapeDtypeStruct(pool.shape, pool.dtype),
        grid_spec=pltpu.PrefetchScalarGridSpec(
            num_scalar_prefetch=2,
            grid=(),
            in_specs=[anywhere] * 3,
            out_specs=anywhere,
            scratch_shapes=[
                pltpu.VMEM((2 * CHUNK,) + pool.shape[1:], pool.dtype),
                pltpu.SemaphoreType.DMA((2,)),
                pltpu.SemaphoreType.DMA,
            ],
        ),
        input_output_aliases={2: 0},
        compiler_params=pltpu.CompilerParams(vmem_limit_bytes=8 << 20),
        name="settle",
    )(table, number, pool, *recv)


def score_kernel(limits, pos_ref, pool_ref, codes_ref, piece_ref, scales_ref, *refs):
    sources, refs = refs[:9], refs[9:]
    bo_ref, out_ref, picked, wide, inter = refs[:5]
    copies, (pick_sem, weight_sem) = refs[5:14], refs[14:]
    w1, w2, w3, w4, b1_ref, b2_ref, b3_ref, b4_ref, wo_ref = copies
    shards, half, count = picked.shape
    tables = shards // 2
    weights = [pltpu.make_async_copy(src, dst, weight_sem.at[n]) for n, (src, dst) in enumerate(zip(sources, copies))]

    slots, piece_base, pool_base, table_row = limits

    def begin(shard, carry):
        e = pos_ref[table_row, shard]
        dest = lax.div(e, jnp.int32(slots))

        @pl.when(e < piece_base)
        def _():
            lanes = pl.ds(pl.multiple_of(dest * count, count), count)
            pltpu.make_async_copy(codes_ref.at[e - dest * slots, :, lanes], picked.at[shard], pick_sem).start()

        @pl.when((e >= piece_base) & (e < pool_base))
        def _():
            pltpu.make_async_copy(piece_ref.at[e - piece_base], picked.at[shard], pick_sem).start()

        @pl.when(e >= pool_base)
        def _():
            pltpu.make_async_copy(pool_ref.at[e - pool_base], picked.at[shard], pick_sem).start()

        return carry

    def finish(shard, carry):
        pltpu.make_async_copy(pool_ref.at[0], picked.at[shard], pick_sem).wait()
        return carry

    def rescale(shard, carry):
        e = pos_ref[table_row, shard]
        dest = lax.div(e, jnp.int32(slots))

        @pl.when(e < piece_base)
        def _():
            lanes = pl.ds(pl.multiple_of(dest * count, count), count)
            factor = scales_ref[pl.ds(e - dest * slots, 1), lanes]
            picked[shard] = (picked[shard].astype(jnp.float32) * factor).astype(picked.dtype)

        return carry

    lax.fori_loop(0, shards, begin, 0)
    for copy in weights:
        copy.start()
    lax.fori_loop(0, shards, finish, 0)
    lax.fori_loop(0, shards, rescale, 0)

    def gram_block(block, carry):
        lanes = pl.ds(pl.multiple_of(block * LANES, LANES), LANES)
        for shard in range(shards):
            wide[shard // 2, (shard % 2) * half:(shard % 2 + 1) * half, :] = picked[shard, :, lanes].astype(jnp.float32)
        row = 0
        for i in range(tables):
            left = wide[i]
            for j in range(i + 1, tables):
                inter[row:row + 1, lanes] = jnp.sum(left * wide[j], axis=0, keepdims=True)
                row += 1
        return carry

    lax.fori_loop(0, count // LANES, gram_block, 0)
    for copy in weights:
        copy.wait()
    step = max(n * LANES for n in (1, 2, 4) if count % (n * LANES) == 0)

    def dense(hidden, weight, bias):
        product = jnp.dot(hidden, weight[...], preferred_element_type=jnp.float32)
        return jnp.maximum(product + bias[...], 0.0).astype(jnp.bfloat16)

    def top_block(block, carry):
        lanes = pl.ds(pl.multiple_of(block * step, step), step)
        hidden = jnp.transpose(inter[:, lanes]).astype(jnp.bfloat16)
        hidden = dense(hidden, w1, b1_ref)
        hidden = dense(hidden, w2, b2_ref)
        hidden = dense(hidden, w3, b3_ref)
        hidden = dense(hidden, w4, b4_ref)
        final = lax.dot_general(wo_ref[...].reshape(1, wo_ref.shape[0]), hidden, (((1,), (1,)), ((), ())), preferred_element_type=jnp.float32)
        out_ref[:, lanes] = final[0:1] + bo_ref[0]
        return carry

    lax.fori_loop(0, count // step, top_block, 0)


def score(pool, codes, piece, scales, positions, shards, limits, layers):
    (w1, b1), (w2, b2), (w3, b3), (w4, b4), (wo, bo) = layers
    half, count = pool.shape[1:]
    rows = w1.shape[0]
    anywhere = pl.BlockSpec(memory_space=pl.ANY)
    vmem = pl.BlockSpec(memory_space=pltpu.VMEM)
    flops = 2 * count * sum(w.size for w in (w1, w2, w3, w4))
    parts = (w1, w2, w3, w4, b1[None, :], b2[None, :], b3[None, :], b4[None, :], wo)
    return pl.pallas_call(
        functools.partial(score_kernel, limits),
        out_shape=jax.ShapeDtypeStruct((1, count), jnp.float32),
        grid_spec=pltpu.PrefetchScalarGridSpec(
            num_scalar_prefetch=1,
            grid=(),
            in_specs=[anywhere] * 3 + [vmem] + [pl.BlockSpec(memory_space=pltpu.HBM)] * 9 + [pl.BlockSpec(memory_space=pltpu.SMEM)],
            out_specs=vmem,
            scratch_shapes=[
                pltpu.VMEM((shards, half, count), pool.dtype),
                pltpu.VMEM((shards // 2, 2 * half, LANES), jnp.float32),
                pltpu.VMEM((rows, count), jnp.float32),
                *(pltpu.VMEM(part.shape, part.dtype) for part in parts),
                pltpu.SemaphoreType.DMA,
                pltpu.SemaphoreType.DMA((len(parts),)),
            ],
        ),
        compiler_params=pltpu.CompilerParams(vmem_limit_bytes=60 << 20),
        cost_estimate=pl.CostEstimate(flops=flops, bytes_accessed=shards * half * count * 2, transcendentals=0),
        name="score",
    )(positions, pool, codes, piece, scales, *parts, bo)


def shard_positions(slot_table, shard_total):
    flat = slot_table.reshape(-1)
    matches = flat[None, :] == jnp.arange(shard_total, dtype=jnp.int32)[:, None]
    places = jnp.arange(flat.shape[0], dtype=jnp.int32)[None, :]
    return jnp.sum(jnp.where(matches, places, 0), axis=1)


def exchange_all(codes, scales):
    slot_count, half, samples = codes.shape
    tbl_count = lax.axis_size("tbl")
    count = samples // tbl_count
    values = (codes.astype(jnp.float32) * scales[:, None, :]).astype(codes.dtype)
    packed = values.reshape(slot_count, half, tbl_count, count).transpose(2, 0, 1, 3)
    received = lax.all_to_all(packed, "tbl", split_axis=0, concat_axis=0, tiled=True)
    return received.reshape(tbl_count * slot_count, half, count)


def exchange_line(code, codes, scales, shard_slot):
    nodes = code.nodes
    _, samples = codes.shape[1:]
    count = samples // (2 * nodes)
    me = lax.axis_index("tbl").astype(jnp.int32)
    table = plan(shard_slot, me[None], code)
    rounds = table[4, 0]

    def index(place, col):
        return place * 2 + col

    swaps = []
    for side in range(2):
        pairs = [(index(a, c), index(a + 1, c)) for a in range(side, nodes - 1, 2) for c in range(2)]
        swaps.append(pairs + [(b, a) for a, b in pairs])
    across = [(index(a, c), index(a, 1 - c)) for a in range(nodes) for c in range(2)]

    def piece(n, after):
        part = column_piece(nodes, n, me[None], codes, scales, after, count)
        return lax.ppermute(part, "tbl", across)

    def swap(sends):
        swapped = []
        for sent, pairs in zip(sends, swaps):
            swapped.append(lax.ppermute(sent, "tbl", pairs))
        return swapped

    def run(limit, open_end):
        return rounds_of(limit, open_end)

    def rounds_of(limit, open_end):
        pool, arrived, pieces = None, [], [piece(0, scales)]
        for r in range(limit):
            ready = [p for n, p in enumerate(pieces[:nodes - 1]) if PIECE_ROUND[n] <= r]
            recv = arrived[r - LAG] if r >= LAG else None
            pool, *sends = turn(code, table, r, codes, scales, ready, pool, recv, count)
            arrived.append(swap(sends))
            if r in PIECE_AFTER[1:]:
                pieces.append(piece(len(pieces), sends[0]))
        final, early, late = jnp.int32(limit), arrived[-2], arrived[-1]
        if open_end:
            pool, early, late, pieces = lax.optimization_barrier((pool, early, late, pieces))

            def step(state):
                r, pool, early, late = state
                pool, *sends = turn(code, table, r[None], codes, scales, pieces[:-1], pool, early, count)
                return r + 1, pool, late, swap(sends)

            final, pool, early, late = lax.while_loop(lambda state: state[0] < rounds, step, (final, pool, early, late))
        pool = settle(table, final[None] - 2, pool, early)
        return settle(table, final[None] - 1, pool, late), pieces[-1]

    steps = [functools.partial(run, limit, limit == ROUND_STEPS[-1]) for limit in ROUND_STEPS]
    choice = sum((rounds > limit).astype(jnp.int32) for limit in ROUND_STEPS[:-1])
    pool, piece_own = lax.switch(choice, steps)
    return table, pool, piece_own


def per_device(codes, scales, shard_slot, *parameters):
    layers = tuple(zip(parameters[0::2], parameters[1::2]))
    slots = codes.shape[0]
    tbl_count = lax.axis_size("tbl")
    shards = 2 * TABLES
    if tbl_count % 4 == 0 and slots >= tbl_count:
        code = Codes(tbl_count // 2, slots)
        places, pool, piece = exchange_line(code, codes, scales, shard_slot)
        limits = (slots, code.piece, code.pool, 5)
    else:
        pool = exchange_all(codes, scales)
        piece, places, limits = pool, shard_positions(shard_slot, shards)[None, :], (slots, 0, 0, 0)
    logits = score(pool, codes, piece, scales, places, shards, limits, layers)
    return lax.all_gather(logits, "pair", axis=0, tiled=True)


def solution(mesh):
    return jax.shard_map(
        per_device,
        mesh=mesh,
        in_specs=(P("tbl", None, "pair"), P("tbl", "pair")) + (P(),) * 11,
        out_specs=P(None, "tbl"),
        check_vma=False,
    )
```
